32 devices in a mesh: seq: 16 (over z, y, core), grp: 2 (over x).
Axes of the slice: x: 2, y: 2, z: 4, core: 2. Of those that a mesh axis runs over, the one named last changes fastest.
Arguments:
- queries: bfloat16 [4096, 2048], P(('seq', 'grp')), may hold values from -6 to 6
- key_vectors: bfloat16 [4096, 2048], P(('seq', 'grp')), may hold values from -6 to 6
- head_value_rows: bfloat16 [4096, 2048], P(('seq', 'grp')), may hold values from -6 to 6
- out_gain: float32 [128], replicated, may hold values from 0.1 to 1.9
Outputs:
- mixed: bfloat16 [4096, 2048], P(('seq', 'grp'))
The draws below stay inside these ranges and needn't reach their ends.
All inputs are finite; a program needn't handle non-finite values.
Results may differ from the reference program's by a relative error of at most 0.0035.
Values may be sent and summed in bfloat16 or wider, within the bound.
No kernel may reach another device: no remote copies, remote signals or barrier semaphores. Data moves between devices by JAX's collectives and lax.ppermute only.
A program may use at most 64 MiB of HBM per device.

```python
import jax
import jax.numpy as jnp
from jax import lax

HEADS = 16
HEAD_DIM = 128
D = 2048
BLOCK = 128
LENGTH = 4096


def steps_of(own_key, dims, shards, smallest, largest):
    level = 1.0
    for axis_at, blocks in shards:
        steps = jax.random.uniform(jax.random.fold_in(jax.random.fold_in(own_key, 6), axis_at), (blocks,), jnp.float32, smallest / len(shards), largest / len(shards))
        level = level * jnp.repeat(jnp.exp(steps), dims[axis_at] // blocks).reshape((-1,) + (1,) * (len(dims) - 1 - axis_at))
    return level


def scatter_about(rng, shape, scale, bound, cuts=(), kind=jnp.bfloat16):
    values = jax.random.normal(rng, shape, jnp.float32) * scale
    if len(cuts) > 0:
        values = steps_of(rng, shape, cuts, -0.22, 0.18) * values
    return jnp.clip(values, min=-bound, max=bound).astype(kind)


def setup_inputs(seed: int = 0) -> dict:
    key_of = jax.random.split(jax.random.key(seed), 5)
    queries = scatter_about(key_of[0], (LENGTH, D), 1.0, 6.0, ((0, 32),))
    key_vectors = scatter_about(key_of[1], (LENGTH, D), 1.0, 6.0, ((0, 32),))
    head_value_rows = scatter_about(key_of[2], (LENGTH, D), 1.0, 6.0, ((0, 32),))
    out_gain = jnp.clip(1.0 + 0.18 * jax.random.normal(key_of[3], (HEAD_DIM,), jnp.float32), 0.1, 1.9)
    return {"queries": queries, "key_vectors": key_vectors, "head_value_rows": head_value_rows, "out_gain": out_gain}


exact_precision = lax.Precision.HIGHEST
key_eps = 1e-06
norm_eps = 1e-05

def block_terms(key_tile_rows, value_block):
    width = key_tile_rows.shape[0]
    strict_lower = jnp.tril(jnp.ones((width, width), jnp.float32), -1)
    inner = jnp.dot(key_tile_rows, key_tile_rows.T, precision=exact_precision)
    system = jnp.eye(width, dtype=jnp.float32) + 2.0 * strict_lower * inner
    stacked = jnp.concatenate([2.0 * key_tile_rows, 2.0 * value_block], axis=1)
    solved = jax.scipy.linalg.solve_triangular(system, stacked, lower=True, unit_diagonal=True)
    half = key_tile_rows.shape[1]
    return (solved[:, :half], solved[:, half:])

def head_output(query_rows, key_rows, value_rows, out_gain):
    query_blocks = query_rows.astype(jnp.float32).reshape(-1, BLOCK, HEAD_DIM)
    raw_keys = key_rows.astype(jnp.float32)
    unit_keys = raw_keys / jnp.sqrt(lax.optimization_barrier(jnp.sum(raw_keys * raw_keys, axis=1, keepdims=True)) + key_eps)
    key_blocks = unit_keys.reshape(-1, BLOCK, HEAD_DIM)
    value_blocks = value_rows.astype(jnp.float32).reshape(-1, BLOCK, HEAD_DIM)
    causal = jnp.tril(jnp.ones((BLOCK, BLOCK), jnp.float32))

    def step_forward(state, pieces):
        query_block, key_tile_rows, value_block = pieces
        key_weights, new_values = block_terms(key_tile_rows, value_block)
        delta = new_values - jnp.dot(key_weights, state, precision=exact_precision)
        scores = causal * jnp.dot(query_block, key_tile_rows.T, precision=exact_precision)
        output = jnp.dot(query_block, state, precision=exact_precision) + jnp.dot(scores, delta, precision=exact_precision)
        return (state + jnp.dot(key_tile_rows.T, delta, precision=exact_precision), output)
    start_state = jnp.zeros((HEAD_DIM, HEAD_DIM), jnp.float32)
    final_state, outputs = lax.scan(step_forward, start_state, (query_blocks, key_blocks, value_blocks))
    outputs = outputs.reshape(-1, HEAD_DIM)
    scale = lax.rsqrt(lax.optimization_barrier(jnp.mean(outputs * outputs, axis=1, keepdims=True)) + norm_eps)
    return (outputs * scale * out_gain).astype(jnp.bfloat16)

def reference(queries, key_vectors, head_value_rows, out_gain):

    def per_head(head_index):
        column_range = (head_index * HEAD_DIM).astype(jnp.int32)
        query_rows = lax.dynamic_slice_in_dim(queries, column_range, HEAD_DIM, 1)
        key_rows = lax.dynamic_slice_in_dim(key_vectors, column_range, HEAD_DIM, 1)
        value_rows = lax.dynamic_slice_in_dim(head_value_rows, column_range, HEAD_DIM, 1)
        return head_output(query_rows, key_rows, value_rows, out_gain)
    mixed = lax.map(per_head, jnp.arange(HEADS, dtype=jnp.int32))
    return mixed.transpose(1, 0, 2).reshape(LENGTH, D)
```

```python
import functools

import jax
import jax.numpy as jnp
from jax import lax
from jax.experimental import pallas as pl
from jax.experimental.pallas import tpu as pltpu
from jax.sharding import Mesh
from jax.sharding import PartitionSpec as P

HEAD_DIM = 128
BLOCK = 128
key_eps = 1e-06
norm_eps = 1e-05
BATCH = 8

f32 = jnp.float32
bf16 = jnp.bfloat16


def mm(left, right):
    return jnp.dot(left, right, preferred_element_type=f32)


def mm_nt(left, right):
    return lax.dot_general(left, right, (((1,), (1,)), ((), ())), preferred_element_type=f32)


def split(value):
    high = value.astype(bf16)
    low = (value - high.astype(f32)).astype(bf16)
    return jnp.concatenate([high, low], axis=1)


def twice(rows):
    return jnp.concatenate([rows, rows], axis=0)


def fold(wide):
    half = wide.shape[1] // 2
    return wide[:, :half] + wide[:, half:]


def product(left_pair, right_pair):
    return fold(mm(left_pair, twice(right_pair)))


def product_wide(left_pair, first_pair, second_pair):
    n = HEAD_DIM
    highs = jnp.concatenate([first_pair[:, :n], second_pair[:, :n]], axis=1)
    lows = jnp.concatenate([first_pair[:, n:], second_pair[:, n:]], axis=1)
    return mm(left_pair, twice(highs)) + mm(left_pair[:, :n], lows)


def iotas():
    row = lax.broadcasted_iota(jnp.int32, (BLOCK, BLOCK), 0)
    col = lax.broadcasted_iota(jnp.int32, (BLOCK, BLOCK), 1)
    return row, col


def batches(count, run):
    size = min(BATCH, count)
    if count == size:
        run([j for j in range(count)])
    else:
        def one(i, carried):
            run([i * size + j for j in range(size)])
            return carried
        lax.fori_loop(0, count // size, one, 0)


def keys_kernel(k_ref, w_ref, tu_ref, a_ref):
    count = k_ref.shape[0]
    row, col = iotas()
    diagonal = row == col
    eye = diagonal.astype(f32)

    def run(blocks):
        keys = [k_ref[j] for j in blocks]
        grams = [mm_nt(k, k) for k in keys]
        coupling, scale_cols, scale_rows = [], [], []
        for g in grams:
            on_diagonal = jnp.where(diagonal, g, 0.0)
            c = 1.0 / jnp.sqrt(jnp.sum(on_diagonal, axis=1, keepdims=True) + key_eps)
            r = 1.0 / jnp.sqrt(jnp.sum(on_diagonal, axis=0, keepdims=True) + key_eps)
            scale_cols.append(c)
            scale_rows.append(r)
            coupling.append(jnp.where(row > col, (2.0 * c) * g * r, 0.0))
        size = 1
        inverses = None
        while size < BLOCK:
            mask = ((row // size) % 2 == 1) & (col // size == row // size - 1)
            parts = [jnp.where(mask, n, 0.0) for n in coupling]
            if inverses is None:
                inverses = [eye - p for p in parts]
            else:
                pairs = [split(t) for t in inverses]
                inner = [product(split(p), t) for p, t in zip(parts, pairs)]
                outer = [product(t, split(z)) for t, z in zip(pairs, inner)]
                inverses = [t - z for t, z in zip(inverses, outer)]
            size *= 2
        for i, j in enumerate(blocks):
            left = (2.0 * scale_cols[i]) * inverses[i]
            tu_ref[j] = split(left)
            weights = mm(split(left * scale_rows[i]), twice(keys[i]))
            weights_pair = split(weights)
            w_ref[j] = weights_pair
            a_ref[j] = split(eye - fold(mm(keys[i].T, weights_pair)))

    batches(count, run)


def tree_offsets(count):
    offsets, at, size = [], 0, count
    while size >= 1:
        offsets.append(at)
        at += size
        size //= 2
    return offsets, at


def values_kernel(k_ref, v_ref, tu_ref, a_leaf_ref, u_ref, a_ref, b_ref, total_ref):
    count = k_ref.shape[0]
    offsets, _ = tree_offsets(count)

    def run(blocks):
        for j in blocks:
            changes = split(mm(tu_ref[j], twice(v_ref[j])))
            u_ref[j] = changes
            a_ref[j] = a_leaf_ref[j]
            b_ref[j] = fold(mm(k_ref[j].T, changes))

    batches(count, run)
    for level in range(1, len(offsets)):
        below, here = offsets[level - 1], offsets[level]
        for i in range(count >> level):
            first, second = below + 2 * i, below + 2 * i + 1
            later = a_ref[second]
            joint = product_wide(later, a_ref[first], split(b_ref[first]))
            a_ref[here + i] = split(joint[:, :HEAD_DIM])
            b_ref[here + i] = joint[:, HEAD_DIM:] + b_ref[second]
    total_ref[...] = b_ref[offsets[-1]]


def queries_kernel(q_ref, k_ref, w_ref, u_ref, a_ref, b_ref, qp_ref, op_ref, pa_ref, pb_ref):
    count = q_ref.shape[0]
    offsets, _ = tree_offsets(count)
    row, col = iotas()
    causal = row >= col
    eye = (row == col).astype(f32)
    levels = len(offsets)
    for level in range(levels - 1, -1, -1):
        here = offsets[level]
        if level == levels - 1:
            pa_ref[here] = split(eye)
            pb_ref[here] = jnp.zeros((HEAD_DIM, HEAD_DIM), f32)
            continue
        above = offsets[level + 1]
        for i in range(count >> (level + 1)):
            left, right, parent = here + 2 * i, here + 2 * i + 1, above + i
            pa_ref[left] = pa_ref[parent]
            pb_ref[left] = pb_ref[parent]
            if i == 0:
                pa_ref[right] = a_ref[left]
                pb_ref[right] = b_ref[left]
            else:
                joint = product_wide(a_ref[left], pa_ref[parent], split(pb_ref[parent]))
                pa_ref[right] = split(joint[:, :HEAD_DIM])
                pb_ref[right] = joint[:, HEAD_DIM:] + b_ref[left]

    def run(blocks):
        scores = [jnp.where(causal, mm_nt(q_ref[j], k_ref[j]), 0.0) for j in blocks]
        local = [product_wide(split(c), w_ref[j], u_ref[j]) for c, j in zip(scores, blocks)]
        for i, j in enumerate(blocks):
            mixed = q_ref[j].astype(f32) - local[i][:, :HEAD_DIM]
            joint = product_wide(split(mixed), pa_ref[j], split(pb_ref[j]))
            qp_ref[j] = split(joint[:, :HEAD_DIM])
            op_ref[j] = joint[:, HEAD_DIM:] + local[i][:, HEAD_DIM:]

    batches(count, run)


def finish_kernel(qp_ref, op_ref, state_ref, gain_ref, out_ref):
    state = twice(split(state_ref[...]))
    gain = gain_ref[...]
    for j in range(qp_ref.shape[0]):
        output = fold(mm(qp_ref[j], state)) + op_ref[j]
        scale = lax.rsqrt(jnp.mean(output * output, axis=1, keepdims=True) + norm_eps)
        out_ref[j] = (output * scale * gain).astype(bf16)


def call(kernel, name, outs, flops, scratch=()):
    vmem = pl.BlockSpec(memory_space=pltpu.VMEM)
    return pl.pallas_call(
        kernel,
        name=name,
        out_shape=tuple(jax.ShapeDtypeStruct(s, t) for s, t in outs),
        out_specs=tuple(vmem for _ in outs),
        scratch_shapes=list(scratch),
        cost_estimate=pl.CostEstimate(flops=flops, bytes_accessed=4 << 20, transcendentals=0),
    )


def body(groups, lanes, queries, key_vectors, head_value_rows, out_gain):
    tokens, features = queries.shape
    heads = features // HEAD_DIM
    blocks = lanes * tokens // BLOCK

    def to_heads(rows):
        pieces = rows.reshape(tokens, heads, HEAD_DIM).transpose(1, 0, 2)
        arrived = lax.all_to_all(pieces, "lo", split_axis=0, concat_axis=0, tiled=True)
        return arrived.reshape(blocks, BLOCK, HEAD_DIM)

    keys = to_heads(key_vectors)
    values = to_heads(head_value_rows)
    query_blocks = to_heads(queries)
    _, nodes = tree_offsets(blocks)
    one = (HEAD_DIM, HEAD_DIM)
    pair = (HEAD_DIM, 2 * HEAD_DIM)
    unit = 2 * BLOCK**3 * 4
    w, tu, a_leaf = call(
        keys_kernel, "keys",
        [((blocks, *pair), bf16), ((blocks, *pair), bf16), ((blocks, *pair), bf16)],
        unit * blocks * 14,
    )(keys)
    u, a, b, total = call(
        values_kernel, "values",
        [((blocks, *pair), bf16), ((nodes, *pair), bf16), ((nodes, *one), f32), (one, f32)],
        unit * blocks * 4,
    )(keys, values, tu, a_leaf)
    hop = [(source, source + 1) for source in range(groups - 1)]
    incoming = lax.ppermute(total, "hi", hop)
    if groups > 2:
        top = a[nodes - 1].astype(f32)
        transition = top[:, :HEAD_DIM] + top[:, HEAD_DIM:]

        def relay(i, arriving):
            leaving = jnp.dot(transition, arriving, precision=lax.Precision.HIGHEST) + total
            return lax.ppermute(leaving, "hi", hop)

        incoming = lax.fori_loop(0, groups - 2, relay, incoming)
    qp, op = call(
        queries_kernel, "queries",
        [((blocks, *pair), bf16), ((blocks, *one), f32)],
        unit * blocks * 6,
        [pltpu.VMEM((nodes, *pair), bf16), pltpu.VMEM((nodes, *one), f32)],
    )(query_blocks, keys, w, u, a, b)
    (out,) = call(
        finish_kernel, "finish", [((blocks, BLOCK, HEAD_DIM), bf16)], unit * blocks,
    )(qp, op, incoming, out_gain.reshape(1, HEAD_DIM))
    back = lax.all_to_all(out.reshape(lanes, tokens, HEAD_DIM), "lo", split_axis=0, concat_axis=0, tiled=True)
    return back.transpose(1, 0, 2).reshape(tokens, features)


def solution(mesh):
    count = mesh.devices.size

    def run(queries, key_vectors, head_value_rows, out_gain):
        lanes = queries.shape[1] // HEAD_DIM
        regrouped = Mesh(mesh.devices.reshape(count // lanes, lanes), ("hi", "lo"))
        rows = P(("hi", "lo"), None)
        return jax.shard_map(
            functools.partial(body, count // lanes, lanes),
            mesh=regrouped, in_specs=(rows, rows, rows, P()), out_specs=rows, check_vma=False,
        )(queries, key_vectors, head_value_rows, out_gain)

    return run
```

```python
import functools

import jax
import jax.numpy as jnp
from jax import lax
from jax.experimental import pallas as pl
from jax.experimental.pallas import tpu as pltpu
from jax.sharding import Mesh
from jax.sharding import PartitionSpec as P

HEAD_DIM = 128
BLOCK = 128
key_eps = 1e-06
norm_eps = 1e-05
BATCH = 8

f32 = jnp.float32
bf16 = jnp.bfloat16


def mm(left, right):
    return jnp.dot(left, right, preferred_element_type=f32)


def mm_nt(left, right):
    return lax.dot_general(left, right, (((1,), (1,)), ((), ())), preferred_element_type=f32)


def split(value):
    high = value.astype(bf16)
    low = (value - high.astype(f32)).astype(bf16)
    return jnp.concatenate([high, low], axis=1)


def twice(rows):
    return jnp.concatenate([rows, rows], axis=0)


def fold(wide):
    half = wide.shape[1] // 2
    return wide[:, :half] + wide[:, half:]


def product(left_pair, right_pair):
    return fold(mm(left_pair, twice(right_pair)))


def product_wide(left_pair, first_pair, second_pair):
    n = HEAD_DIM
    highs = jnp.concatenate([first_pair[:, :n], second_pair[:, :n]], axis=1)
    lows = jnp.concatenate([first_pair[:, n:], second_pair[:, n:]], axis=1)
    return mm(left_pair, twice(highs)) + mm(left_pair[:, :n], lows)


def iotas():
    row = lax.broadcasted_iota(jnp.int32, (BLOCK, BLOCK), 0)
    col = lax.broadcasted_iota(jnp.int32, (BLOCK, BLOCK), 1)
    return row, col


def batches(count, run):
    size = min(BATCH, count)
    if count == size:
        run([j for j in range(count)])
    else:
        def one(i, carried):
            run([i * size + j for j in range(size)])
            return carried
        lax.fori_loop(0, count // size, one, 0)


def node_offsets(count):
    offsets, at, size = [], 0, count
    while size >= 1:
        offsets.append(at)
        at += size
        size //= 2
    return offsets, at


def pack_kernel(*refs):
    *ins, out_ref = refs
    for i, ref in enumerate(ins):
        for h in range(out_ref.shape[0]):
            out_ref[h, i] = ref[:, h * HEAD_DIM : (h + 1) * HEAD_DIM]


def unpack_kernel(in_ref, out_ref):
    for h in range(in_ref.shape[0]):
        out_ref[:, h * HEAD_DIM : (h + 1) * HEAD_DIM] = in_ref[h]


def keys_kernel(k_ref, w_ref, tu_ref, a_ref, pa_ref):
    count = k_ref.shape[0]
    offsets, _ = node_offsets(count)
    row, col = iotas()
    diagonal = row == col
    eye = diagonal.astype(f32)

    def run(blocks):
        keys = [k_ref[j, 0] for j in blocks]
        grams = [mm_nt(k, k) for k in keys]
        coupling, scale_cols, scale_rows = [], [], []
        for g in grams:
            on_diagonal = jnp.where(diagonal, g, 0.0)
            c = 1.0 / jnp.sqrt(jnp.sum(on_diagonal, axis=1, keepdims=True) + key_eps)
            r = 1.0 / jnp.sqrt(jnp.sum(on_diagonal, axis=0, keepdims=True) + key_eps)
            scale_cols.append(c)
            scale_rows.append(r)
            coupling.append(jnp.where(row > col, (2.0 * c) * g * r, 0.0))
        size = 1
        inverses = None
        while size < BLOCK:
            mask = ((row // size) % 2 == 1) & (col // size == row // size - 1)
            parts = [jnp.where(mask, n, 0.0) for n in coupling]
            if inverses is None:
                inverses = [eye - p for p in parts]
            else:
                pairs = [split(t) for t in inverses]
                inner = [product(split(p), t) for p, t in zip(parts, pairs)]
                outer = [product(t, split(z)) for t, z in zip(pairs, inner)]
                inverses = [t - z for t, z in zip(inverses, outer)]
            size *= 2
        for i, j in enumerate(blocks):
            left = (2.0 * scale_cols[i]) * inverses[i]
            tu_ref[j] = split(left)
            weights = split(mm(split(left * scale_rows[i]), twice(keys[i])))
            w_ref[j] = weights
            a_ref[j] = split(eye - fold(mm(keys[i].T, weights)))

    batches(count, run)
    for level in range(1, len(offsets)):
        below, here = offsets[level - 1], offsets[level]
        for i in range(count >> level):
            a_ref[here + i] = split(product(a_ref[below + 2 * i + 1], a_ref[below + 2 * i]))
    for (target, left, parent) in prefix_steps(count):
        if parent is None:
            pa_ref[target] = split(eye) if left is None else a_ref[left]
        elif left is None:
            pa_ref[target] = pa_ref[parent]
        else:
            pa_ref[target] = split(product(a_ref[left], pa_ref[parent]))


def prefix_steps(count):
    offsets, _ = node_offsets(count)
    steps = []
    for level in range(len(offsets) - 2, -1, -1):
        here, above = offsets[level], offsets[level + 1]
        for i in range(count >> (level + 1)):
            parent = above + i if i > 0 else None
            if i > 0 or level == 0:
                steps.append((here + 2 * i, None, parent))
            steps.append((here + 2 * i + 1, here + 2 * i, parent))
    return steps


def values_kernel(k_ref, vq_ref, tu_ref, a_ref, u_ref, b_ref, total_ref):
    count = k_ref.shape[0]
    offsets, _ = node_offsets(count)

    def run(blocks):
        changes = [split(mm(tu_ref[j], twice(vq_ref[j, 0]))) for j in blocks]
        for i, j in enumerate(blocks):
            u_ref[j] = changes[i]
            b_ref[j] = fold(mm(k_ref[j, 0].T, changes[i]))

    batches(count, run)
    for level in range(1, len(offsets)):
        below, here = offsets[level - 1], offsets[level]
        for i in range(count >> level):
            first, second = below + 2 * i, below + 2 * i + 1
            b_ref[here + i] = product(a_ref[second], split(b_ref[first])) + b_ref[second]
    total_ref[...] = b_ref[offsets[-1]]


def queries_kernel(k_ref, vq_ref, w_ref, u_ref, a_ref, b_ref, qt_ref, ol_ref, pb_ref):
    count = k_ref.shape[0]
    row, col = iotas()
    causal = row >= col

    def run(blocks):
        scores = [jnp.where(causal, mm_nt(vq_ref[j, 1], k_ref[j, 0]), 0.0) for j in blocks]
        local = [product_wide(split(c), w_ref[j], u_ref[j]) for c, j in zip(scores, blocks)]
        for i, j in enumerate(blocks):
            qt_ref[j] = split(vq_ref[j, 1].astype(f32) - local[i][:, :HEAD_DIM])
            ol_ref[j] = local[i][:, HEAD_DIM:]

    batches(count, run)
    for (target, left, parent) in prefix_steps(count):
        if parent is None:
            pb_ref[target] = jnp.zeros((HEAD_DIM, HEAD_DIM), f32) if left is None else b_ref[left]
        elif left is None:
            pb_ref[target] = pb_ref[parent]
        else:
            pb_ref[target] = product(a_ref[left], split(pb_ref[parent])) + b_ref[left]


def finish_kernel(qt_ref, ol_ref, pa_ref, pb_ref, state_ref, gain_ref, out_ref):
    arrived = jnp.where(lax.axis_index("hi") > 0, state_ref[...], 0.0)
    state = twice(split(arrived))
    gain = gain_ref[...]

    def run(blocks):
        starts = [fold(mm(pa_ref[j], state)) + pb_ref[j] for j in blocks]
        outputs = [product(qt_ref[j], split(s)) + ol_ref[j] for j, s in zip(blocks, starts)]
        for j, output in zip(blocks, outputs):
            scale = lax.rsqrt(jnp.mean(output * output, axis=1, keepdims=True) + norm_eps)
            out_ref[j] = (output * scale * gain).astype(bf16)

    batches(out_ref.shape[0], run)


def call(kernel, name, outs, flops, kept=True, limit=24 << 20):
    vmem = pl.BlockSpec(memory_space=pltpu.VMEM)
    make = pltpu.VMEM if kept else jax.ShapeDtypeStruct
    return pl.pallas_call(
        kernel,
        name=name,
        out_shape=tuple(make(s, t) for s, t in outs),
        out_specs=tuple(vmem for _ in outs),
        compiler_params=pltpu.CompilerParams(vmem_limit_bytes=limit),
        cost_estimate=pl.CostEstimate(flops=flops, bytes_accessed=4 << 20, transcendentals=0),
    )


def near(*values):
    return [pltpu.with_memory_space_constraint(v, pltpu.VMEM) for v in values]


def body(groups, lanes, queries, key_vectors, head_value_rows, out_gain):
    tokens, features = queries.shape
    if tokens != BLOCK or features != lanes * HEAD_DIM:
        raise ValueError("unsupported sizes")
    blocks = lanes

    def to_heads(*rows):
        shape = (lanes, len(rows), BLOCK, HEAD_DIM)
        (pieces,) = call(pack_kernel, "pack", [(shape, bf16)], 0, kept=False)(*rows)
        return lax.all_to_all(pieces, "lo", split_axis=0, concat_axis=0, tiled=True)

    keys = to_heads(key_vectors)
    vq = to_heads(head_value_rows, queries)
    _, nodes = node_offsets(blocks)
    one = (HEAD_DIM, HEAD_DIM)
    pair = (HEAD_DIM, 2 * HEAD_DIM)
    unit = 2 * BLOCK**3 * 4
    w, tu, a, pa = call(
        keys_kernel, "keys",
        [((blocks, *pair), bf16), ((blocks, *pair), bf16), ((nodes, *pair), bf16), ((nodes, *pair), bf16)],
        unit * blocks * 20,
    )(keys)
    u, b, total = call(
        values_kernel, "values",
        [((blocks, *pair), bf16), ((nodes, *one), f32), (one, f32)],
        unit * blocks * 4,
    )(keys, vq, *near(tu, a))
    hop = [(source, (source + 1) % groups) for source in range(groups)]
    incoming = lax.ppermute(total, "hi", hop)
    if groups > 2:
        top = a[nodes - 1].astype(f32)
        transition = top[:, :HEAD_DIM] + top[:, HEAD_DIM:]

        def relay(i, arriving):
            arriving = jnp.where(lax.axis_index("hi") > 0, arriving, 0.0)
            leaving = jnp.dot(transition, arriving, precision=lax.Precision.HIGHEST) + total
            return lax.ppermute(leaving, "hi", hop)

        incoming = lax.fori_loop(0, groups - 2, relay, incoming)
    qt, ol, pb = call(
        queries_kernel, "queries",
        [((blocks, *pair), bf16), ((blocks, *one), f32), ((nodes, *one), f32)],
        unit * blocks * 6,
    )(keys, vq, *near(w, u, a, b))
    (out,) = call(
        finish_kernel, "finish", [((blocks, BLOCK, HEAD_DIM), bf16)], unit * blocks * 2, kept=False,
    )(*near(qt, ol, pa, pb), incoming, out_gain.reshape(1, HEAD_DIM))
    back = lax.all_to_all(out, "lo", split_axis=0, concat_axis=0, tiled=True)
    (mixed,) = call(unpack_kernel, "unpack", [((tokens, features), bf16)], 0, kept=False)(back)
    return mixed


def solution(mesh):
    count = mesh.devices.size

    def run(queries, key_vectors, head_value_rows, out_gain):
        lanes = queries.shape[1] // HEAD_DIM
        regrouped = Mesh(mesh.devices.reshape(count // lanes, lanes), ("hi", "lo"))
        rows = P(("hi", "lo"), None)
        return jax.shard_map(
            functools.partial(body, count // lanes, lanes),
            mesh=regrouped, in_specs=(rows, rows, rows, P()), out_specs=rows, check_vma=False,
        )(queries, key_vectors, head_value_rows, out_gain)

    return run
```

```python
import functools

import jax
import jax.numpy as jnp
from jax import lax
from jax.experimental import pallas as pl
from jax.experimental.pallas import tpu as pltpu
from jax.sharding import Mesh
from jax.sharding import PartitionSpec as P

HEAD_DIM = 128
BLOCK = 128
key_eps = 1e-06
norm_eps = 1e-05
BATCH = 8

f32 = jnp.float32
bf16 = jnp.bfloat16


def mm(left, right):
    return jnp.dot(left, right, preferred_element_type=f32)


def mm_nt(left, right):
    return lax.dot_general(left, right, (((1,), (1,)), ((), ())), preferred_element_type=f32)


def split(value):
    high = value.astype(bf16)
    low = (value - high.astype(f32)).astype(bf16)
    return jnp.concatenate([high, low], axis=1)


def twice(rows):
    return jnp.concatenate([rows, rows], axis=0)


def fold(wide):
    half = wide.shape[1] // 2
    return wide[:, :half] + wide[:, half:]


def product(left_pair, right_pair):
    return fold(mm(left_pair, twice(right_pair)))


def product_wide(left_pair, first_pair, second_pair):
    n = HEAD_DIM
    highs = jnp.concatenate([first_pair[:, :n], second_pair[:, :n]], axis=1)
    lows = jnp.concatenate([first_pair[:, n:], second_pair[:, n:]], axis=1)
    return mm(left_pair, twice(highs)) + mm(left_pair[:, :n], lows)


def iotas():
    row = lax.broadcasted_iota(jnp.int32, (BLOCK, BLOCK), 0)
    col = lax.broadcasted_iota(jnp.int32, (BLOCK, BLOCK), 1)
    return row, col


def batches(count, run):
    size = min(BATCH, count)
    if count == size:
        run([j for j in range(count)])
    else:
        def one(i, carried):
            run([i * size + j for j in range(size)])
            return carried
        lax.fori_loop(0, count // size, one, 0)


def node_offsets(count):
    offsets, at, size = [], 0, count
    while size >= 1:
        offsets.append(at)
        at += size
        size //= 2
    return offsets, at


def pack_kernel(*refs):
    *ins, out_ref = refs
    for i, ref in enumerate(ins):
        for h in range(out_ref.shape[0]):
            out_ref[h, i] = ref[:, h * HEAD_DIM : (h + 1) * HEAD_DIM]


def unpack_kernel(in_ref, out_ref):
    for h in range(in_ref.shape[0]):
        out_ref[:, h * HEAD_DIM : (h + 1) * HEAD_DIM] = in_ref[h]


def keys_kernel(kvq_ref, w_ref, tu_ref, a_ref, pa_ref):
    count = kvq_ref.shape[0]
    offsets, _ = node_offsets(count)
    row, col = iotas()
    diagonal = row == col
    eye = diagonal.astype(f32)

    def run(blocks):
        keys = [kvq_ref[j, 0] for j in blocks]
        grams = [mm_nt(k, k) for k in keys]
        coupling, scale_cols, scale_rows = [], [], []
        for g in grams:
            on_diagonal = jnp.where(diagonal, g, 0.0)
            c = 1.0 / jnp.sqrt(jnp.sum(on_diagonal, axis=1, keepdims=True) + key_eps)
            r = 1.0 / jnp.sqrt(jnp.sum(on_diagonal, axis=0, keepdims=True) + key_eps)
            scale_cols.append(c)
            scale_rows.append(r)
            coupling.append(jnp.where(row > col, (2.0 * c) * g * r, 0.0))
        size = 1
        inverses = None
        while size < BLOCK:
            mask = ((row // size) % 2 == 1) & (col // size == row // size - 1)
            parts = [jnp.where(mask, n, 0.0) for n in coupling]
            if inverses is None:
                inverses = [eye - p for p in parts]
            else:
                pairs = [split(t) for t in inverses]
                inner = [product(split(p), t) for p, t in zip(parts, pairs)]
                outer = [product(t, split(z)) for t, z in zip(pairs, inner)]
                inverses = [t - z for t, z in zip(inverses, outer)]
            size *= 2
        for i, j in enumerate(blocks):
            left = (2.0 * scale_cols[i]) * inverses[i]
            tu_ref[j] = split(left)
            weights = split(mm(split(left * scale_rows[i]), twice(keys[i])))
            w_ref[j] = weights
            a_ref[j] = split(eye - fold(mm(keys[i].T, weights)))

    batches(count, run)
    for level in range(1, len(offsets)):
        below, here = offsets[level - 1], offsets[level]
        for i in range(count >> level):
            a_ref[here + i] = split(product(a_ref[below + 2 * i + 1], a_ref[below + 2 * i]))
    for (target, left, parent) in prefix_steps(count):
        if parent is None:
            pa_ref[target] = split(eye) if left is None else a_ref[left]
        elif left is None:
            pa_ref[target] = pa_ref[parent]
        else:
            pa_ref[target] = split(product(a_ref[left], pa_ref[parent]))


def prefix_steps(count):
    offsets, _ = node_offsets(count)
    steps = []
    for level in range(len(offsets) - 2, -1, -1):
        here, above = offsets[level], offsets[level + 1]
        for i in range(count >> (level + 1)):
            parent = above + i if i > 0 else None
            if i > 0 or level == 0:
                steps.append((here + 2 * i, None, parent))
            steps.append((here + 2 * i + 1, here + 2 * i, parent))
    return steps


def values_kernel(kvq_ref, tu_ref, a_ref, u_ref, b_ref, total_ref):
    count = kvq_ref.shape[0]
    offsets, _ = node_offsets(count)

    def run(blocks):
        changes = [split(mm(tu_ref[j], twice(kvq_ref[j, 1]))) for j in blocks]
        for i, j in enumerate(blocks):
            u_ref[j] = changes[i]
            b_ref[j] = fold(mm(kvq_ref[j, 0].T, changes[i]))

    batches(count, run)
    for level in range(1, len(offsets)):
        below, here = offsets[level - 1], offsets[level]
        for i in range(count >> level):
            first, second = below + 2 * i, below + 2 * i + 1
            b_ref[here + i] = product(a_ref[second], split(b_ref[first])) + b_ref[second]
    total_ref[...] = b_ref[offsets[-1]]


def queries_kernel(kvq_ref, w_ref, u_ref, a_ref, b_ref, qt_ref, ol_ref, pb_ref):
    count = kvq_ref.shape[0]
    row, col = iotas()
    causal = row >= col

    def run(blocks):
        scores = [jnp.where(causal, mm_nt(kvq_ref[j, 2], kvq_ref[j, 0]), 0.0) for j in blocks]
        local = [product_wide(split(c), w_ref[j], u_ref[j]) for c, j in zip(scores, blocks)]
        for i, j in enumerate(blocks):
            qt_ref[j] = split(kvq_ref[j, 2].astype(f32) - local[i][:, :HEAD_DIM])
            ol_ref[j] = local[i][:, HEAD_DIM:]

    batches(count, run)
    for (target, left, parent) in prefix_steps(count):
        if parent is None:
            pb_ref[target] = jnp.zeros((HEAD_DIM, HEAD_DIM), f32) if left is None else b_ref[left]
        elif left is None:
            pb_ref[target] = pb_ref[parent]
        else:
            pb_ref[target] = product(a_ref[left], split(pb_ref[parent])) + b_ref[left]


def finish_kernel(qt_ref, ol_ref, pa_ref, pb_ref, state_ref, gain_ref, out_ref):
    arrived = jnp.where(lax.axis_index("hi") > 0, state_ref[...], 0.0)
    state = twice(split(arrived))
    gain = gain_ref[...]

    def run(blocks):
        starts = [fold(mm(pa_ref[j], state)) + pb_ref[j] for j in blocks]
        outputs = [product(qt_ref[j], split(s)) + ol_ref[j] for j, s in zip(blocks, starts)]
        for j, output in zip(blocks, outputs):
            scale = lax.rsqrt(jnp.mean(output * output, axis=1, keepdims=True) + norm_eps)
            out_ref[j] = (output * scale * gain).astype(bf16)

    batches(out_ref.shape[0], run)


def call(kernel, name, outs, flops, kept=True, limit=24 << 20):
    vmem = pl.BlockSpec(memory_space=pltpu.VMEM)
    make = pltpu.VMEM if kept else jax.ShapeDtypeStruct
    return pl.pallas_call(
        kernel,
        name=name,
        out_shape=tuple(make(s, t) for s, t in outs),
        out_specs=tuple(vmem for _ in outs),
        compiler_params=pltpu.CompilerParams(vmem_limit_bytes=limit),
        cost_estimate=pl.CostEstimate(flops=flops, bytes_accessed=4 << 20, transcendentals=0),
    )


def near(*values):
    return [pltpu.with_memory_space_constraint(v, pltpu.VMEM) for v in values]


def body(groups, lanes, queries, key_vectors, head_value_rows, out_gain):
    tokens, features = queries.shape
    if tokens != BLOCK or features != lanes * HEAD_DIM:
        raise ValueError("unsupported sizes")
    blocks = lanes

    def to_heads(*rows):
        shape = (lanes, len(rows), BLOCK, HEAD_DIM)
        (pieces,) = call(pack_kernel, "pack", [(shape, bf16)], 0, kept=False)(*rows)
        return lax.all_to_all(pieces, "lo", split_axis=0, concat_axis=0, tiled=True)

    kvq = to_heads(key_vectors, head_value_rows, queries)
    _, nodes = node_offsets(blocks)
    one = (HEAD_DIM, HEAD_DIM)
    pair = (HEAD_DIM, 2 * HEAD_DIM)
    unit = 2 * BLOCK**3 * 4
    w, tu, a, pa = call(
        keys_kernel, "keys",
        [((blocks, *pair), bf16), ((blocks, *pair), bf16), ((nodes, *pair), bf16), ((nodes, *pair), bf16)],
        unit * blocks * 20,
    )(*near(kvq))
    u, b, total = call(
        values_kernel, "values",
        [((blocks, *pair), bf16), ((nodes, *one), f32), (one, f32)],
        unit * blocks * 4,
    )(*near(kvq, tu, a))
    hop = [(source, (source + 1) % groups) for source in range(groups)]
    incoming = lax.ppermute(total, "hi", hop)
    if groups > 2:
        top = a[nodes - 1].astype(f32)
        transition = top[:, :HEAD_DIM] + top[:, HEAD_DIM:]

        def relay(i, arriving):
            arriving = jnp.where(lax.axis_index("hi") > 0, arriving, 0.0)
            leaving = jnp.dot(transition, arriving, precision=lax.Precision.HIGHEST) + total
            return lax.ppermute(leaving, "hi", hop)

        incoming = lax.fori_loop(0, groups - 2, relay, incoming)
    qt, ol, pb = call(
        queries_kernel, "queries",
        [((blocks, *pair), bf16), ((blocks, *one), f32), ((nodes, *one), f32)],
        unit * blocks * 6,
    )(*near(kvq, w, u, a, b))
    (out,) = call(
        finish_kernel, "finish", [((blocks, BLOCK, HEAD_DIM), bf16)], unit * blocks * 2, kept=False,
    )(*near(qt, ol, pa, pb), incoming, out_gain.reshape(1, HEAD_DIM))
    back = lax.all_to_all(out, "lo", split_axis=0, concat_axis=0, tiled=True)
    (mixed,) = call(unpack_kernel, "unpack", [((tokens, features), bf16)], 0, kept=False)(back)
    return mixed


def solution(mesh):
    count = mesh.devices.size

    def run(queries, key_vectors, head_value_rows, out_gain):
        lanes = queries.shape[1] // HEAD_DIM
        regrouped = Mesh(mesh.devices.reshape(count // lanes, lanes), ("hi", "lo"))
        rows = P(("hi", "lo"), None)
        return jax.shard_map(
            functools.partial(body, count // lanes, lanes),
            mesh=regrouped, in_specs=(rows, rows, rows, P()), out_specs=rows, check_vma=False,
        )(queries, key_vectors, head_value_rows, out_gain)

    return run
```

```python
import functools

import jax
import jax.numpy as jnp
from jax import lax
from jax.experimental import pallas as pl
from jax.experimental.pallas import tpu as pltpu
from jax.sharding import Mesh
from jax.sharding import PartitionSpec as P

HEAD_DIM = 128
BLOCK = 128
key_eps = 1e-06
norm_eps = 1e-05
BATCH = 8
BASE = 8

f32 = jnp.float32
bf16 = jnp.bfloat16


def mm(left, right):
    return jnp.dot(left, right, preferred_element_type=f32)


def mm_nt(left, right):
    return lax.dot_general(left, right, (((1,), (1,)), ((), ())), preferred_element_type=f32)


def split(value):
    high = value.astype(bf16)
    low = (value - high.astype(f32)).astype(bf16)
    return jnp.concatenate([high, low], axis=1)


def twice(rows):
    return jnp.concatenate([rows, rows], axis=0)


def fold(wide):
    half = wide.shape[1] // 2
    return wide[:, :half] + wide[:, half:]


def product(left_pair, right_pair):
    return fold(mm(left_pair, twice(right_pair)))


def product_wide(left_pair, first_pair, second_pair):
    n = HEAD_DIM
    highs = jnp.concatenate([first_pair[:, :n], second_pair[:, :n]], axis=1)
    lows = jnp.concatenate([first_pair[:, n:], second_pair[:, n:]], axis=1)
    return mm(left_pair, twice(highs)) + mm(left_pair[:, :n], lows)


def iotas():
    row = lax.broadcasted_iota(jnp.int32, (BLOCK, BLOCK), 0)
    col = lax.broadcasted_iota(jnp.int32, (BLOCK, BLOCK), 1)
    return row, col


def batches(count, run):
    size = min(BATCH, count)
    if count == size:
        run([j for j in range(count)])
    else:
        def one(i, carried):
            run([i * size + j for j in range(size)])
            return carried
        lax.fori_loop(0, count // size, one, 0)


def node_offsets(count):
    offsets, at, size = [], 0, count
    while size >= 1:
        offsets.append(at)
        at += size
        size //= 2
    return offsets, at


def move(pairs, sem):
    copies = [pltpu.make_async_copy(source, target, sem.at[i]) for i, (source, target) in enumerate(pairs)]
    for copy in copies:
        copy.start()
    for copy in copies:
        copy.wait()


def columns(h):
    return pl.ds(h * HEAD_DIM, HEAD_DIM)


def pack_kernel(*refs):
    *ins, out_ref, sem = refs
    heads = out_ref.shape[0]
    move([(ref.at[:, columns(h)], out_ref.at[h, i]) for i, ref in enumerate(ins) for h in range(heads)], sem)


def unpack_kernel(in_ref, out_ref, sem):
    move([(in_ref.at[h], out_ref.at[:, columns(h)]) for h in range(in_ref.shape[0])], sem)


def base_inverses(coupling):
    count, tiles, lanes = len(coupling), BLOCK // BASE, BLOCK
    tile = lax.broadcasted_iota(jnp.int32, (tiles, BASE, lanes), 0)
    lane = lax.broadcasted_iota(jnp.int32, (tiles, BASE, lanes), 2)
    own = lane // BASE == tile
    packed = [jnp.sum(jnp.where(own, n.reshape(tiles, BASE, lanes), 0.0), axis=0) for n in coupling]
    rows = split(jnp.concatenate(packed, axis=0))
    source = lax.broadcasted_iota(jnp.int32, (lanes, lanes), 0)
    target = lax.broadcasted_iota(jnp.int32, (lanes, lanes), 1)
    same = source // BASE == target // BASE
    spread = jnp.concatenate(
        [(same & (source % BASE == k)).astype(bf16) for k in range(BASE - 1)], axis=1
    )
    factors = mm(rows, twice(spread))
    sub = lax.broadcasted_iota(jnp.int32, (count, BASE, lanes), 1)
    at = lax.broadcasted_iota(jnp.int32, (count, BASE, lanes), 2) % BASE
    solved = (sub == at).astype(f32)
    for k in range(BASE - 1):
        factor = factors[:, k * lanes : (k + 1) * lanes].reshape(count, BASE, lanes)
        solved = solved - factor * solved[:, k : k + 1, :]
    return [
        jnp.where(own, jnp.broadcast_to(solved[i][None], (tiles, BASE, lanes)), 0.0).reshape(BLOCK, lanes)
        for i in range(count)
    ]


def maps_kernel(climb, kvq_ref, w_ref, u_ref, a_ref, b_ref, total_ref):
    count = kvq_ref.shape[0]
    offsets, _ = node_offsets(count)
    row, col = iotas()
    diagonal = row == col
    eye = diagonal.astype(f32)

    def run(blocks):
        keys = [kvq_ref[j, 0] for j in blocks]
        grams = [mm_nt(k, k) for k in keys]
        coupling, scale_cols, scale_rows = [], [], []
        for g in grams:
            on_diagonal = jnp.where(diagonal, g, 0.0)
            c = 1.0 / jnp.sqrt(jnp.sum(on_diagonal, axis=1, keepdims=True) + key_eps)
            r = 1.0 / jnp.sqrt(jnp.sum(on_diagonal, axis=0, keepdims=True) + key_eps)
            scale_cols.append(c)
            scale_rows.append(r)
            coupling.append(jnp.where(row > col, (2.0 * c) * g * r, 0.0))
        inverses = base_inverses(coupling)
        size = BASE
        while size < BLOCK:
            mask = ((row // size) % 2 == 1) & (col // size == row // size - 1)
            parts = [jnp.where(mask, n, 0.0) for n in coupling]
            pairs = [split(t) for t in inverses]
            inner = [product(split(p), t) for p, t in zip(parts, pairs)]
            outer = [product(t, split(z)) for t, z in zip(pairs, inner)]
            inverses = [t - z for t, z in zip(inverses, outer)]
            size *= 2
        lefts = [(2.0 * c) * t for c, t in zip(scale_cols, inverses)]
        weights = [split(mm(split(t * r), twice(k))) for t, r, k in zip(lefts, scale_rows, keys)]
        changes = [split(mm(split(t), twice(kvq_ref[j, 1]))) for t, j in zip(lefts, blocks)]
        for i, j in enumerate(blocks):
            w_ref[j] = weights[i]
            u_ref[j] = changes[i]
            across = keys[i].T
            a_ref[j] = split(eye - fold(mm(across, weights[i])))
            b_ref[j] = fold(mm(across, changes[i]))

    batches(count, run)
    for level in range(1, len(offsets)):
        below, here = offsets[level - 1], offsets[level]
        for i in range(count >> level):
            first, second = below + 2 * i, below + 2 * i + 1
            later = a_ref[second]
            b_ref[here + i] = product(later, split(b_ref[first])) + b_ref[second]
            if climb or level < len(offsets) - 1:
                a_ref[here + i] = split(product(later, a_ref[first]))
    total_ref[...] = b_ref[offsets[-1]]


def prefix_steps(count):
    offsets, _ = node_offsets(count)
    steps = []
    for level in range(len(offsets) - 2, -1, -1):
        here, above = offsets[level], offsets[level + 1]
        for i in range(count >> (level + 1)):
            parent = above + i if i > 0 else None
            if i > 0 or level == 0:
                steps.append((here + 2 * i, None, parent))
            steps.append((here + 2 * i + 1, here + 2 * i, parent))
    return steps


def queries_kernel(kvq_ref, w_ref, u_ref, a_ref, b_ref, qp_ref, op_ref, pa_ref, pb_ref):
    count = kvq_ref.shape[0]
    row, col = iotas()
    causal = row >= col
    for (target, left, parent) in prefix_steps(count):
        if parent is None:
            pa_ref[target] = split((row == col).astype(f32)) if left is None else a_ref[left]
            pb_ref[target] = jnp.zeros((HEAD_DIM, HEAD_DIM), f32) if left is None else b_ref[left]
        elif left is None:
            pa_ref[target] = pa_ref[parent]
            pb_ref[target] = pb_ref[parent]
        else:
            pa_ref[target] = split(product(a_ref[left], pa_ref[parent]))
            pb_ref[target] = product(a_ref[left], split(pb_ref[parent])) + b_ref[left]

    def run(blocks):
        scores = [jnp.where(causal, mm_nt(kvq_ref[j, 2], kvq_ref[j, 0]), 0.0) for j in blocks]
        local = [product_wide(split(c), w_ref[j], u_ref[j]) for c, j in zip(scores, blocks)]
        through = [split(kvq_ref[j, 2].astype(f32) - t[:, :HEAD_DIM]) for t, j in zip(local, blocks)]
        joint = [product_wide(t, pa_ref[j], split(pb_ref[j])) for t, j in zip(through, blocks)]
        for i, j in enumerate(blocks):
            qp_ref[j] = split(joint[i][:, :HEAD_DIM])
            op_ref[j] = joint[i][:, HEAD_DIM:] + local[i][:, HEAD_DIM:]

    batches(count, run)


def finish_kernel(qp_ref, op_ref, state_ref, gain_ref, out_ref):
    arrived = jnp.where(lax.axis_index("hi") > 0, state_ref[...], 0.0)
    state = twice(split(arrived))
    gain = gain_ref[...]

    def run(blocks):
        outputs = [fold(mm(qp_ref[j], state)) + op_ref[j] for j in blocks]
        for j, output in zip(blocks, outputs):
            scale = lax.rsqrt(jnp.mean(output * output, axis=1, keepdims=True) + norm_eps)
            out_ref[j] = (output * scale * gain).astype(bf16)

    batches(out_ref.shape[0], run)


def call(kernel, name, outs, flops, kept=True, limit=24 << 20, scratch=(), in_space=None):
    vmem = pl.BlockSpec(memory_space=pltpu.VMEM)
    far = pl.BlockSpec(memory_space=pltpu.HBM)
    make = pltpu.VMEM if kept else jax.ShapeDtypeStruct
    extra = {} if in_space is None else {"in_specs": [pl.BlockSpec(memory_space=s) for s in in_space]}
    return pl.pallas_call(
        kernel,
        name=name,
        out_shape=tuple(make(s, t) for s, t in outs),
        out_specs=tuple(vmem if kept else far for _ in outs),
        scratch_shapes=list(scratch),
        compiler_params=pltpu.CompilerParams(vmem_limit_bytes=limit),
        cost_estimate=pl.CostEstimate(flops=flops, bytes_accessed=4 << 20, transcendentals=0),
        **extra,
    )


def held(space, *values):
    return [pltpu.with_memory_space_constraint(v, space) for v in values]


def near(*values):
    return held(pltpu.VMEM, *values)


def body(groups, lanes, queries, key_vectors, head_value_rows, out_gain):
    tokens, features = queries.shape
    if tokens != BLOCK or features != lanes * HEAD_DIM:
        raise ValueError("unsupported sizes")
    blocks = lanes
    _, nodes = node_offsets(blocks)
    one = (HEAD_DIM, HEAD_DIM)
    pair = (HEAD_DIM, 2 * HEAD_DIM)
    unit = 2 * BLOCK**3 * 4
    dma = pltpu.SemaphoreType.DMA
    pieces_shape = (lanes, 3, BLOCK, HEAD_DIM)
    (pieces,) = call(
        pack_kernel, "pack", [(pieces_shape, bf16)], 0, scratch=[dma((3 * lanes,))], in_space=[pltpu.HBM] * 3,
    )(*held(pltpu.HBM, key_vectors, head_value_rows, queries))
    kvq = lax.all_to_all(pieces, "lo", split_axis=0, concat_axis=0, tiled=True)
    w, u, a, b, total = call(
        functools.partial(maps_kernel, groups > 2), "maps",
        [((blocks, *pair), bf16), ((blocks, *pair), bf16), ((nodes, *pair), bf16), ((nodes, *one), f32), (one, f32)],
        unit * blocks * 20,
    )(*near(kvq))
    hop = [(source, (source + 1) % groups) for source in range(groups)]
    incoming = lax.ppermute(total, "hi", hop)
    if groups > 2:
        top = a[nodes - 1].astype(f32)
        transition = top[:, :HEAD_DIM] + top[:, HEAD_DIM:]

        def relay(i, arriving):
            arriving = jnp.where(lax.axis_index("hi") > 0, arriving, 0.0)
            leaving = jnp.dot(transition, arriving, precision=lax.Precision.HIGHEST) + total
            return lax.ppermute(leaving, "hi", hop)

        incoming = lax.fori_loop(0, groups - 2, relay, incoming)
    qp, op = call(
        queries_kernel, "queries",
        [((blocks, *pair), bf16), ((blocks, *one), f32)],
        unit * blocks * 6,
        scratch=[pltpu.VMEM((nodes, *pair), bf16), pltpu.VMEM((nodes, *one), f32)],
    )(*near(kvq, w, u, a, b))
    (out,) = call(
        finish_kernel, "finish", [((blocks, BLOCK, HEAD_DIM), bf16)], unit * blocks * 2,
    )(*near(qp, op), incoming, out_gain.reshape(1, HEAD_DIM))
    back = lax.all_to_all(out, "lo", split_axis=0, concat_axis=0, tiled=True)
    (mixed,) = call(
        unpack_kernel, "unpack", [((tokens, features), bf16)], 0, kept=False, scratch=[dma((lanes,))],
    )(*near(back))
    return mixed


def solution(mesh):
    count = mesh.devices.size

    def run(queries, key_vectors, head_value_rows, out_gain):
        lanes = queries.shape[1] // HEAD_DIM
        regrouped = Mesh(mesh.devices.reshape(count // lanes, lanes), ("hi", "lo"))
        rows = P(("hi", "lo"), None)
        return jax.shard_map(
            functools.partial(body, count // lanes, lanes),
            mesh=regrouped, in_specs=(rows, rows, rows, P()), out_specs=rows, check_vma=False,
        )(queries, key_vectors, head_value_rows, out_gain)

    return run
```

```python
import functools

import jax
import jax.numpy as jnp
from jax import lax
from jax.experimental import pallas as pl
from jax.experimental.pallas import tpu as pltpu
from jax.sharding import Mesh
from jax.sharding import PartitionSpec as P

HEAD_DIM = 128
BLOCK = 128
key_eps = 1e-06
norm_eps = 1e-05
BATCH = 16
BASE = 16
PARTS = 4

f32 = jnp.float32
bf16 = jnp.bfloat16


def mm(left, right):
    return jnp.dot(left, right, preferred_element_type=f32)


def mm_nt(left, right):
    return lax.dot_general(left, right, (((1,), (1,)), ((), ())), preferred_element_type=f32)


def split(value):
    high = value.astype(bf16)
    low = (value - high.astype(f32)).astype(bf16)
    return jnp.concatenate([high, low], axis=1)


def twice(rows):
    return jnp.concatenate([rows, rows], axis=0)


def fold(wide):
    half = wide.shape[1] // 2
    return wide[:, :half] + wide[:, half:]


def stack(first_pair, second_pair):
    n = HEAD_DIM
    highs = jnp.concatenate([first_pair[:, :n], second_pair[:, :n]], axis=1)
    lows = jnp.concatenate([first_pair[:, n:], second_pair[:, n:]], axis=1)
    return jnp.concatenate([highs, lows], axis=0)


def product(left_pair, right_pair):
    return fold(mm(left_pair, twice(right_pair)))


def product_wide(left_pair, first_pair, second_pair):
    n = HEAD_DIM
    highs = jnp.concatenate([first_pair[:, :n], second_pair[:, :n]], axis=1)
    lows = jnp.concatenate([first_pair[:, n:], second_pair[:, n:]], axis=1)
    return mm(left_pair, twice(highs)) + mm(left_pair[:, :n], lows)


def iotas():
    row = lax.broadcasted_iota(jnp.int32, (BLOCK, BLOCK), 0)
    col = lax.broadcasted_iota(jnp.int32, (BLOCK, BLOCK), 1)
    return row, col


def batches(count, run):
    size = min(BATCH, count)
    if count == size:
        run([j for j in range(count)])
    else:
        def one(i, carried):
            run([i * size + j for j in range(size)])
            return carried
        lax.fori_loop(0, count // size, one, 0)


def node_offsets(count):
    offsets, at, size = [], 0, count
    while size >= 1:
        offsets.append(at)
        at += size
        size //= 2
    return offsets, at


def pack_kernel(*refs):
    *ins, out_ref, held_ref, sem = refs
    copies = [pltpu.make_async_copy(ref, held_ref.at[i], sem.at[i]) for i, ref in enumerate(ins)]
    for copy in copies:
        copy.start()
    for i, copy in enumerate(copies):
        copy.wait()
        for h in range(out_ref.shape[0]):
            out_ref[h, i] = held_ref[i, :, h * HEAD_DIM : (h + 1) * HEAD_DIM]


def unpack_kernel(in_ref, out_ref, held_ref, sem):
    size = out_ref.shape[0] // PARTS
    copies = []
    for i in range(PARTS):
        rows = slice(i * size, (i + 1) * size)
        for h in range(in_ref.shape[0]):
            held_ref[rows, h * HEAD_DIM : (h + 1) * HEAD_DIM] = in_ref[h, rows]
        copies.append(pltpu.make_async_copy(held_ref.at[rows], out_ref.at[rows], sem.at[i]))
        copies[-1].start()
    for copy in copies:
        copy.wait()


def base_inverses(coupling):
    count, tiles, lanes = len(coupling), BLOCK // BASE, BLOCK
    tile = lax.broadcasted_iota(jnp.int32, (tiles, BASE, lanes), 0)
    lane = lax.broadcasted_iota(jnp.int32, (tiles, BASE, lanes), 2)
    own = lane // BASE == tile
    packed = [jnp.sum(jnp.where(own, n.reshape(tiles, BASE, lanes), 0.0), axis=0) for n in coupling]
    rows = split(jnp.concatenate(packed, axis=0))
    source = lax.broadcasted_iota(jnp.int32, (lanes, lanes), 0)
    target = lax.broadcasted_iota(jnp.int32, (lanes, lanes), 1)
    same = source // BASE == target // BASE
    spread = jnp.concatenate(
        [(same & (source % BASE == k)).astype(bf16) for k in range(BASE - 1)], axis=1
    )
    factors = mm(rows, twice(spread))
    sub = lax.broadcasted_iota(jnp.int32, (count, BASE, lanes), 1)
    at = lax.broadcasted_iota(jnp.int32, (count, BASE, lanes), 2) % BASE
    solved = (sub == at).astype(f32)
    for k in range(BASE - 1):
        factor = factors[:, k * lanes : (k + 1) * lanes].reshape(count, BASE, lanes)
        solved = solved - factor * solved[:, k : k + 1, :]
    return [
        jnp.where(own, jnp.broadcast_to(solved[i][None], (tiles, BASE, lanes)), 0.0).reshape(BLOCK, lanes)
        for i in range(count)
    ]


def maps_kernel(climb, kvq_ref, w_ref, u_ref, a_ref, b_ref, total_ref):
    count = kvq_ref.shape[0]
    offsets, _ = node_offsets(count)
    row, col = iotas()
    diagonal = row == col
    eye = diagonal.astype(f32)

    def run(blocks):
        keys = [kvq_ref[j, 0] for j in blocks]
        grams = [mm_nt(k, k) for k in keys]
        coupling, scale_cols, scale_rows = [], [], []
        for g in grams:
            on_diagonal = jnp.where(diagonal, g, 0.0)
            c = 1.0 / jnp.sqrt(jnp.sum(on_diagonal, axis=1, keepdims=True) + key_eps)
            r = 1.0 / jnp.sqrt(jnp.sum(on_diagonal, axis=0, keepdims=True) + key_eps)
            scale_cols.append(c)
            scale_rows.append(r)
            coupling.append(jnp.where(row > col, (2.0 * c) * g * r, 0.0))
        inverses = base_inverses(coupling)
        size = BASE
        while size < BLOCK:
            mask = ((row // size) % 2 == 1) & (col // size == row // size - 1)
            parts = [jnp.where(mask, n, 0.0) for n in coupling]
            pairs = [split(t) for t in inverses]
            inner = [product(split(p), t) for p, t in zip(parts, pairs)]
            outer = [product(t, split(z)) for t, z in zip(pairs, inner)]
            inverses = [t - z for t, z in zip(inverses, outer)]
            size *= 2
        lefts = [(2.0 * c) * t for c, t in zip(scale_cols, inverses)]
        weights = [split(mm(split(t * r), twice(k))) for t, r, k in zip(lefts, scale_rows, keys)]
        changes = [split(mm(split(t), twice(kvq_ref[j, 1]))) for t, j in zip(lefts, blocks)]
        for i, j in enumerate(blocks):
            w_ref[j] = weights[i]
            u_ref[j] = changes[i]
            across = keys[i].T
            both = mm(jnp.concatenate([across, across], axis=1), stack(weights[i], changes[i]))
            a_ref[j] = split(eye - both[:, :HEAD_DIM])
            b_ref[j] = both[:, HEAD_DIM:]

    batches(count, run)
    for level in range(1, len(offsets)):
        below, here = offsets[level - 1], offsets[level]
        for i in range(count >> level):
            first, second = below + 2 * i, below + 2 * i + 1
            later = a_ref[second]
            b_ref[here + i] = product(later, split(b_ref[first])) + b_ref[second]
            if climb or level < len(offsets) - 1:
                a_ref[here + i] = split(product(later, a_ref[first]))
    total_ref[...] = b_ref[offsets[-1]]


def prefix_steps(count):
    offsets, _ = node_offsets(count)
    steps = []
    for level in range(len(offsets) - 2, -1, -1):
        here, above = offsets[level], offsets[level + 1]
        for i in range(count >> (level + 1)):
            parent = above + i if i > 0 else None
            if i > 0 or level == 0:
                steps.append((here + 2 * i, None, parent))
            steps.append((here + 2 * i + 1, here + 2 * i, parent))
    return steps


def queries_kernel(kvq_ref, w_ref, u_ref, a_ref, b_ref, qp_ref, op_ref, pa_ref, pb_ref):
    count = kvq_ref.shape[0]
    row, col = iotas()
    causal = row >= col
    for (target, left, parent) in prefix_steps(count):
        if parent is None:
            pa_ref[target] = split((row == col).astype(f32)) if left is None else a_ref[left]
            pb_ref[target] = jnp.zeros((HEAD_DIM, HEAD_DIM), f32) if left is None else b_ref[left]
        elif left is None:
            pa_ref[target] = pa_ref[parent]
            pb_ref[target] = pb_ref[parent]
        else:
            pa_ref[target] = split(product(a_ref[left], pa_ref[parent]))
            pb_ref[target] = product(a_ref[left], split(pb_ref[parent])) + b_ref[left]

    def run(blocks):
        scores = [jnp.where(causal, mm_nt(kvq_ref[j, 2], kvq_ref[j, 0]), 0.0) for j in blocks]
        local = [product_wide(split(c), w_ref[j], u_ref[j]) for c, j in zip(scores, blocks)]
        through = [split(kvq_ref[j, 2].astype(f32) - t[:, :HEAD_DIM]) for t, j in zip(local, blocks)]
        joint = [product_wide(t, pa_ref[j], split(pb_ref[j])) for t, j in zip(through, blocks)]
        for i, j in enumerate(blocks):
            qp_ref[j] = split(joint[i][:, :HEAD_DIM])
            op_ref[j] = joint[i][:, HEAD_DIM:] + local[i][:, HEAD_DIM:]

    batches(count, run)


def finish_kernel(qp_ref, op_ref, state_ref, gain_ref, out_ref):
    arrived = jnp.where(lax.axis_index("hi") > 0, state_ref[...], 0.0)
    state = twice(split(arrived))
    gain = gain_ref[...]

    def run(blocks):
        outputs = [fold(mm(qp_ref[j], state)) + op_ref[j] for j in blocks]
        for j, output in zip(blocks, outputs):
            scale = lax.rsqrt(jnp.mean(output * output, axis=1, keepdims=True) + norm_eps)
            out_ref[j] = (output * scale * gain).astype(bf16)

    batches(out_ref.shape[0], run)


def call(kernel, name, outs, flops, kept=True, limit=24 << 20, scratch=(), in_space=None):
    vmem = pl.BlockSpec(memory_space=pltpu.VMEM)
    far = pl.BlockSpec(memory_space=pltpu.HBM)
    make = pltpu.VMEM if kept else jax.ShapeDtypeStruct
    extra = {} if in_space is None else {"in_specs": [pl.BlockSpec(memory_space=s) for s in in_space]}
    return pl.pallas_call(
        kernel,
        name=name,
        out_shape=tuple(make(s, t) for s, t in outs),
        out_specs=tuple(vmem if kept else far for _ in outs),
        scratch_shapes=list(scratch),
        compiler_params=pltpu.CompilerParams(vmem_limit_bytes=limit),
        cost_estimate=pl.CostEstimate(flops=flops, bytes_accessed=4 << 20, transcendentals=0),
        **extra,
    )


def held(space, *values):
    return [pltpu.with_memory_space_constraint(v, space) for v in values]


def near(*values):
    return held(pltpu.VMEM, *values)


def body(groups, lanes, queries, key_vectors, head_value_rows, out_gain):
    tokens, features = queries.shape
    if tokens != BLOCK or features != lanes * HEAD_DIM:
        raise ValueError("unsupported sizes")
    blocks = lanes
    _, nodes = node_offsets(blocks)
    one = (HEAD_DIM, HEAD_DIM)
    pair = (HEAD_DIM, 2 * HEAD_DIM)
    unit = 2 * BLOCK**3 * 4
    dma = pltpu.SemaphoreType.DMA
    pieces_shape = (lanes, 3, BLOCK, HEAD_DIM)
    (pieces,) = call(
        pack_kernel, "pack", [(pieces_shape, bf16)], 0, scratch=[pltpu.VMEM((3, tokens, features), bf16), dma((3,))], in_space=[pltpu.HBM] * 3,
    )(*held(pltpu.HBM, key_vectors, head_value_rows, queries))
    kvq = lax.all_to_all(pieces, "lo", split_axis=0, concat_axis=0, tiled=True)
    w, u, a, b, total = call(
        functools.partial(maps_kernel, groups > 2), "maps",
        [((blocks, *pair), bf16), ((blocks, *pair), bf16), ((nodes, *pair), bf16), ((nodes, *one), f32), (one, f32)],
        unit * blocks * 20,
    )(*near(kvq))
    hop = [(source, (source + 1) % groups) for source in range(groups)]
    incoming = lax.ppermute(total, "hi", hop)
    if groups > 2:
        top = a[nodes - 1].astype(f32)
        transition = top[:, :HEAD_DIM] + top[:, HEAD_DIM:]

        def relay(i, arriving):
            arriving = jnp.where(lax.axis_index("hi") > 0, arriving, 0.0)
            leaving = jnp.dot(transition, arriving, precision=lax.Precision.HIGHEST) + total
            return lax.ppermute(leaving, "hi", hop)

        incoming = lax.fori_loop(0, groups - 2, relay, incoming)
    qp, op = call(
        queries_kernel, "queries",
        [((blocks, *pair), bf16), ((blocks, *one), f32)],
        unit * blocks * 6,
        scratch=[pltpu.VMEM((nodes, *pair), bf16), pltpu.VMEM((nodes, *one), f32)],
    )(*near(kvq, w, u, a, b))
    (out,) = call(
        finish_kernel, "finish", [((blocks, BLOCK, HEAD_DIM), bf16)], unit * blocks * 2,
    )(*near(qp, op), incoming, out_gain.reshape(1, HEAD_DIM))
    back = lax.all_to_all(out, "lo", split_axis=0, concat_axis=0, tiled=True)
    (mixed,) = call(
        unpack_kernel, "unpack", [((tokens, features), bf16)], 0, kept=False, scratch=[pltpu.VMEM((tokens, features), bf16), dma((PARTS,))],
    )(*near(back))
    return mixed


def solution(mesh):
    count = mesh.devices.size

    def run(queries, key_vectors, head_value_rows, out_gain):
        lanes = queries.shape[1] // HEAD_DIM
        regrouped = Mesh(mesh.devices.reshape(count // lanes, lanes), ("hi", "lo"))
        rows = P(("hi", "lo"), None)
        return jax.shard_map(
            functools.partial(body, count // lanes, lanes),
            mesh=regrouped, in_specs=(rows, rows, rows, P()), out_specs=rows, check_vma=False,
        )(queries, key_vectors, head_value_rows, out_gain)

    return run
```

```python
import functools

import jax
import jax.numpy as jnp
from jax import lax
from jax.experimental import pallas as pl
from jax.experimental.pallas import tpu as pltpu
from jax.sharding import Mesh
from jax.sharding import PartitionSpec as P

HEAD_DIM = 128
BLOCK = 128
key_eps = 1e-06
norm_eps = 1e-05
BATCH = 16
BASE = 16
PARTS = 4

f32 = jnp.float32
bf16 = jnp.bfloat16


def mm(left, right):
    return jnp.dot(left, right, preferred_element_type=f32)


def mm_nt(left, right):
    return lax.dot_general(left, right, (((1,), (1,)), ((), ())), preferred_element_type=f32)


def split(value):
    high = value.astype(bf16)
    low = (value - high.astype(f32)).astype(bf16)
    return jnp.concatenate([high, low], axis=1)


def twice(rows):
    return jnp.concatenate([rows, rows], axis=0)


def fold(wide):
    half = wide.shape[1] // 2
    return wide[:, :half] + wide[:, half:]


def stack(first_pair, second_pair):
    n = HEAD_DIM
    highs = jnp.concatenate([first_pair[:, :n], second_pair[:, :n]], axis=1)
    lows = jnp.concatenate([first_pair[:, n:], second_pair[:, n:]], axis=1)
    return jnp.concatenate([highs, lows], axis=0)


def product(left_pair, right_pair):
    return fold(mm(left_pair, twice(right_pair)))


def product_wide(left_pair, first_pair, second_pair):
    n = HEAD_DIM
    highs = jnp.concatenate([first_pair[:, :n], second_pair[:, :n]], axis=1)
    lows = jnp.concatenate([first_pair[:, n:], second_pair[:, n:]], axis=1)
    return mm(left_pair, twice(highs)) + mm(left_pair[:, :n], lows)


def iotas():
    row = lax.broadcasted_iota(jnp.int32, (BLOCK, BLOCK), 0)
    col = lax.broadcasted_iota(jnp.int32, (BLOCK, BLOCK), 1)
    return row, col


def batches(count, run):
    size = min(BATCH, count)
    if count == size:
        run([j for j in range(count)])
    else:
        def one(i, carried):
            run([i * size + j for j in range(size)])
            return carried
        lax.fori_loop(0, count // size, one, 0)


def node_offsets(count):
    offsets, at, size = [], 0, count
    while size >= 1:
        offsets.append(at)
        at += size
        size //= 2
    return offsets, at


def pack_kernel(*refs):
    *ins, out_ref, held_ref, sem = refs
    copies = [pltpu.make_async_copy(ref, held_ref.at[i], sem.at[i]) for i, ref in enumerate(ins)]
    for copy in copies:
        copy.start()
    for i, copy in enumerate(copies):
        copy.wait()
        for h in range(out_ref.shape[0]):
            out_ref[h, i] = held_ref[i, :, h * HEAD_DIM : (h + 1) * HEAD_DIM]


def unpack_kernel(in_ref, out_ref, held_ref, sem):
    size = out_ref.shape[0] // PARTS
    copies = []
    for i in range(PARTS):
        rows = slice(i * size, (i + 1) * size)
        for h in range(in_ref.shape[0]):
            held_ref[rows, h * HEAD_DIM : (h + 1) * HEAD_DIM] = in_ref[h, rows]
        copies.append(pltpu.make_async_copy(held_ref.at[rows], out_ref.at[rows], sem.at[i]))
        copies[-1].start()
    for copy in copies:
        copy.wait()


def base_inverses(coupling):
    count, tiles, lanes = len(coupling), BLOCK // BASE, BLOCK
    tile = lax.broadcasted_iota(jnp.int32, (tiles, BASE, lanes), 0)
    lane = lax.broadcasted_iota(jnp.int32, (tiles, BASE, lanes), 2)
    own = lane // BASE == tile
    packed = [jnp.sum(jnp.where(own, n.reshape(tiles, BASE, lanes), 0.0), axis=0) for n in coupling]
    rows = split(jnp.concatenate(packed, axis=0))
    source = lax.broadcasted_iota(jnp.int32, (lanes, lanes), 0)
    target = lax.broadcasted_iota(jnp.int32, (lanes, lanes), 1)
    same = source // BASE == target // BASE
    spread = jnp.concatenate(
        [(same & (source % BASE == k)).astype(bf16) for k in range(BASE - 1)], axis=1
    )
    factors = mm(rows, twice(spread))
    sub = lax.broadcasted_iota(jnp.int32, (count, BASE, lanes), 1)
    at = lax.broadcasted_iota(jnp.int32, (count, BASE, lanes), 2) % BASE
    solved = (sub == at).astype(f32)
    for k in range(BASE - 1):
        factor = factors[:, k * lanes : (k + 1) * lanes].reshape(count, BASE, lanes)
        solved = solved - factor * solved[:, k : k + 1, :]
    return [
        jnp.where(own, jnp.broadcast_to(solved[i][None], (tiles, BASE, lanes)), 0.0).reshape(BLOCK, lanes)
        for i in range(count)
    ]


def maps_kernel(climb, kvq_ref, k_ref, w_ref, u_far, a_ref, b_ref, total_ref, u_ref, sem):
    count = kvq_ref.shape[0]
    park = pltpu.make_async_copy(u_ref, u_far, sem.at[0])
    offsets, _ = node_offsets(count)
    row, col = iotas()
    diagonal = row == col
    eye = diagonal.astype(f32)

    def run(blocks):
        keys = [kvq_ref[j, 0] for j in blocks]
        grams = [mm_nt(k, k) for k in keys]
        coupling, scale_cols, scale_rows = [], [], []
        for g in grams:
            on_diagonal = jnp.where(diagonal, g, 0.0)
            c = 1.0 / jnp.sqrt(jnp.sum(on_diagonal, axis=1, keepdims=True) + key_eps)
            r = 1.0 / jnp.sqrt(jnp.sum(on_diagonal, axis=0, keepdims=True) + key_eps)
            scale_cols.append(c)
            scale_rows.append(r)
            coupling.append(jnp.where(row > col, (2.0 * c) * g * r, 0.0))
        inverses = base_inverses(coupling)
        size = BASE
        while size < BLOCK:
            mask = ((row // size) % 2 == 1) & (col // size == row // size - 1)
            parts = [jnp.where(mask, n, 0.0) for n in coupling]
            pairs = [split(t) for t in inverses]
            inner = [product(split(p), t) for p, t in zip(parts, pairs)]
            outer = [product(t, split(z)) for t, z in zip(pairs, inner)]
            inverses = [t - z for t, z in zip(inverses, outer)]
            size *= 2
        lefts = [(2.0 * c) * t for c, t in zip(scale_cols, inverses)]
        weights = [split(mm(split(t * r), twice(k))) for t, r, k in zip(lefts, scale_rows, keys)]
        changes = [split(mm(split(t), twice(kvq_ref[j, 1]))) for t, j in zip(lefts, blocks)]
        for i, j in enumerate(blocks):
            u_ref[j] = changes[i]
        park.start()
        for i, j in enumerate(blocks):
            k_ref[j] = keys[i]
            w_ref[j] = weights[i]
            across = keys[i].T
            both = mm(jnp.concatenate([across, across], axis=1), stack(weights[i], changes[i]))
            a_ref[j] = split(eye - both[:, :HEAD_DIM])
            b_ref[j] = both[:, HEAD_DIM:]

    run(range(count))
    for level in range(1, len(offsets)):
        below, here = offsets[level - 1], offsets[level]
        for i in range(count >> level):
            first, second = below + 2 * i, below + 2 * i + 1
            later = a_ref[second]
            b_ref[here + i] = product(later, split(b_ref[first])) + b_ref[second]
            if climb or level < len(offsets) - 1:
                a_ref[here + i] = split(product(later, a_ref[first]))
    total_ref[...] = b_ref[offsets[-1]]
    park.wait()


def prefix_steps(count):
    offsets, _ = node_offsets(count)
    steps = []
    for level in range(len(offsets) - 2, -1, -1):
        here, above = offsets[level], offsets[level + 1]
        for i in range(count >> (level + 1)):
            parent = above + i if i > 0 else None
            if i > 0 or level == 0:
                steps.append((here + 2 * i, None, parent))
            steps.append((here + 2 * i + 1, here + 2 * i, parent))
    return steps


def sweep_kernel(a_ref, b_ref, pa_out, pb_out, pa_ref, pb_ref, sem):
    count = pa_out.shape[0]
    row, col = iotas()
    copies = []
    for (target, left, parent) in prefix_steps(count):
        if parent is None:
            pa_ref[target] = split((row == col).astype(f32)) if left is None else a_ref[left]
            pb_ref[target] = jnp.zeros((HEAD_DIM, HEAD_DIM), f32) if left is None else b_ref[left]
        elif left is None:
            pa_ref[target] = pa_ref[parent]
            pb_ref[target] = pb_ref[parent]
        else:
            pa_ref[target] = split(product(a_ref[left], pa_ref[parent]))
            pb_ref[target] = product(a_ref[left], split(pb_ref[parent])) + b_ref[left]
    leaves = pl.ds(0, count)
    copies = [
        pltpu.make_async_copy(pa_ref.at[leaves], pa_out, sem.at[0]),
        pltpu.make_async_copy(pb_ref.at[leaves], pb_out, sem.at[1]),
    ]
    for copy in copies:
        copy.start()
    for copy in copies:
        copy.wait()


def queries_kernel(q_ref, k_ref, w_ref, u_far, pa_far, pb_far, qp_ref, op_ref, u_ref, pa_ref, pb_ref, sem):
    count = k_ref.shape[0]
    row, col = iotas()
    causal = row >= col
    loads = [(u_far, u_ref), (pa_far, pa_ref), (pb_far, pb_ref)]
    copies = [pltpu.make_async_copy(source, target, sem.at[i]) for i, (source, target) in enumerate(loads)]
    for copy in copies:
        copy.start()
    blocks = range(count)
    scores = [split(jnp.where(causal, mm_nt(q_ref[j, 0], k_ref[j]), 0.0)) for j in blocks]
    through = [split(q_ref[j, 0].astype(f32) - product(c, w_ref[j])) for c, j in zip(scores, blocks)]
    copies[0].wait()
    local = [product(c, u_ref[j]) for c, j in zip(scores, blocks)]
    for copy in copies[1:]:
        copy.wait()
    joint = [product_wide(t, pa_ref[j], split(pb_ref[j])) for t, j in zip(through, blocks)]
    for j in blocks:
        qp_ref[j] = split(joint[j][:, :HEAD_DIM])
        op_ref[j] = joint[j][:, HEAD_DIM:] + local[j]


def finish_kernel(qp_ref, op_ref, state_ref, gain_ref, out_ref):
    arrived = jnp.where(lax.axis_index("hi") > 0, state_ref[...], 0.0)
    state = twice(split(arrived))
    gain = gain_ref[...]

    def run(blocks):
        outputs = [fold(mm(qp_ref[j], state)) + op_ref[j] for j in blocks]
        for j, output in zip(blocks, outputs):
            scale = lax.rsqrt(jnp.mean(output * output, axis=1, keepdims=True) + norm_eps)
            out_ref[j] = (output * scale * gain).astype(bf16)

    batches(out_ref.shape[0], run)


def call(kernel, name, outs, flops, kept=True, limit=24 << 20, scratch=(), in_space=None):
    spaces = [pltpu.VMEM if kept is True or i in (kept or ()) else pltpu.HBM for i in range(len(outs))]
    extra = {} if in_space is None else {"in_specs": [pl.BlockSpec(memory_space=s) for s in in_space]}
    return pl.pallas_call(
        kernel,
        name=name,
        out_shape=tuple(space(s, t) for space, (s, t) in zip(spaces, outs)),
        out_specs=tuple(pl.BlockSpec(memory_space=space) for space in spaces),
        scratch_shapes=list(scratch),
        compiler_params=pltpu.CompilerParams(vmem_limit_bytes=limit),
        cost_estimate=pl.CostEstimate(flops=flops, bytes_accessed=4 << 20, transcendentals=0),
        **extra,
    )


def held(space, *values):
    return [pltpu.with_memory_space_constraint(v, space) for v in values]


def near(*values):
    return held(pltpu.VMEM, *values)


def far(*values):
    return held(pltpu.HBM, *values)


def body(groups, lanes, queries, key_vectors, head_value_rows, out_gain):
    tokens, features = queries.shape
    if tokens != BLOCK or features != lanes * HEAD_DIM:
        raise ValueError("unsupported sizes")
    blocks = lanes
    _, nodes = node_offsets(blocks)
    one = (HEAD_DIM, HEAD_DIM)
    pair = (HEAD_DIM, 2 * HEAD_DIM)
    unit = 2 * BLOCK**3 * 4
    dma = pltpu.SemaphoreType.DMA

    def to_heads(*rows):
        count = len(rows)
        (pieces,) = call(
            pack_kernel, "pack", [((lanes, count, BLOCK, HEAD_DIM), bf16)], 0,
            scratch=[pltpu.VMEM((count, tokens, features), bf16), dma((count,))], in_space=[pltpu.HBM] * count,
        )(*far(*rows))
        return lax.all_to_all(pieces, "lo", split_axis=0, concat_axis=0, tiled=True)

    with jax.named_scope("kvmove"):
        kv = to_heads(key_vectors, head_value_rows)
    with jax.named_scope("qmove"):
        q = to_heads(queries)
    with jax.named_scope("maps"):
        k, w, u, a, b, total = call(
            functools.partial(maps_kernel, groups > 2), "maps",
            [((blocks, *one), bf16), ((blocks, *pair), bf16), ((blocks, *pair), bf16),
             ((nodes, *pair), bf16), ((nodes, *one), f32), (one, f32)],
            unit * blocks * 20, kept=(0, 1, 3, 4, 5),
            scratch=[pltpu.VMEM((blocks, *pair), bf16), dma((1,))],
        )(*near(kv))
    hop = [(source, (source + 1) % groups) for source in range(groups)]
    with jax.named_scope("hop"):
        incoming = lax.ppermute(total, "hi", hop)
    if groups > 2:
        top = a[nodes - 1].astype(f32)
        transition = top[:, :HEAD_DIM] + top[:, HEAD_DIM:]

        def relay(i, arriving):
            arriving = jnp.where(lax.axis_index("hi") > 0, arriving, 0.0)
            leaving = jnp.dot(transition, arriving, precision=lax.Precision.HIGHEST) + total
            return lax.ppermute(leaving, "hi", hop)

        incoming = lax.fori_loop(0, groups - 2, relay, incoming)
    prefixes = [((blocks, *pair), bf16), ((blocks, *one), f32)]
    with jax.named_scope("sweep"):
        pa, pb = call(
            sweep_kernel, "sweep", prefixes, unit * blocks * 2, kept=False,
            scratch=[pltpu.VMEM((nodes, *pair), bf16), pltpu.VMEM((nodes, *one), f32), dma((2,))],
        )(*near(a, b))
    qp, op = call(
        queries_kernel, "queries", [((blocks, *pair), bf16), ((blocks, *one), f32)], unit * blocks * 6,
        scratch=[pltpu.VMEM((blocks, *pair), bf16)] + [pltpu.VMEM(s, t) for s, t in prefixes] + [dma((3,))],
        in_space=[pltpu.VMEM] * 3 + [pltpu.HBM] * 3,
    )(*near(q, k, w), *far(u, pa, pb))
    (out,) = call(
        finish_kernel, "finish", [((blocks, BLOCK, HEAD_DIM), bf16)], unit * blocks * 2,
    )(*near(qp, op), incoming, out_gain.reshape(1, HEAD_DIM))
    back = lax.all_to_all(out, "lo", split_axis=0, concat_axis=0, tiled=True)
    (mixed,) = call(
        unpack_kernel, "unpack", [((tokens, features), bf16)], 0, kept=False,
        scratch=[pltpu.VMEM((tokens, features), bf16), dma((PARTS,))],
    )(*near(back))
    return mixed


def solution(mesh):
    count = mesh.devices.size

    def run(queries, key_vectors, head_value_rows, out_gain):
        lanes = queries.shape[1] // HEAD_DIM
        regrouped = Mesh(mesh.devices.reshape(count // lanes, lanes), ("hi", "lo"))
        rows = P(("hi", "lo"), None)
        return jax.shard_map(
            functools.partial(body, count // lanes, lanes),
            mesh=regrouped, in_specs=(rows, rows, rows, P()), out_specs=rows, check_vma=False,
        )(queries, key_vectors, head_value_rows, out_gain)

    return run
```

```python
import functools

import jax
import jax.numpy as jnp
from jax import lax
from jax.experimental import pallas as pl
from jax.experimental.pallas import tpu as pltpu
from jax.sharding import Mesh
from jax.sharding import PartitionSpec as P

HEAD_DIM = 128
BLOCK = 128
key_eps = 1e-06
norm_eps = 1e-05
BATCH = 16
BASE = 16
PARTS = 4

f32 = jnp.float32
bf16 = jnp.bfloat16


def mm(left, right):
    return jnp.dot(left, right, preferred_element_type=f32)


def mm_nt(left, right):
    return lax.dot_general(left, right, (((1,), (1,)), ((), ())), preferred_element_type=f32)


def split(value):
    high = value.astype(bf16)
    low = (value - high.astype(f32)).astype(bf16)
    return jnp.concatenate([high, low], axis=1)


def twice(rows):
    return jnp.concatenate([rows, rows], axis=0)


def fold(wide):
    half = wide.shape[1] // 2
    return wide[:, :half] + wide[:, half:]


def stack(first_pair, second_pair):
    n = HEAD_DIM
    highs = jnp.concatenate([first_pair[:, :n], second_pair[:, :n]], axis=1)
    lows = jnp.concatenate([first_pair[:, n:], second_pair[:, n:]], axis=1)
    return jnp.concatenate([highs, lows], axis=0)


def product(left_pair, right_pair):
    return fold(mm(left_pair, twice(right_pair)))


def product_wide(left_pair, first_pair, second_pair):
    n = HEAD_DIM
    highs = jnp.concatenate([first_pair[:, :n], second_pair[:, :n]], axis=1)
    lows = jnp.concatenate([first_pair[:, n:], second_pair[:, n:]], axis=1)
    return mm(left_pair, twice(highs)) + mm(left_pair[:, :n], lows)


def iotas():
    row = lax.broadcasted_iota(jnp.int32, (BLOCK, BLOCK), 0)
    col = lax.broadcasted_iota(jnp.int32, (BLOCK, BLOCK), 1)
    return row, col


def batches(count, run):
    size = min(BATCH, count)
    if count == size:
        run([j for j in range(count)])
    else:
        def one(i, carried):
            run([i * size + j for j in range(size)])
            return carried
        lax.fori_loop(0, count // size, one, 0)


def node_offsets(count):
    offsets, at, size = [], 0, count
    while size >= 1:
        offsets.append(at)
        at += size
        size //= 2
    return offsets, at


def pack_kernel(q_ref, k_ref, v_ref, kv_ref, q_far, rows_ref, moved_ref, sem):
    ins = (q_ref, k_ref, v_ref)
    copies = [pltpu.make_async_copy(ref, rows_ref.at[i], sem.at[i]) for i, ref in enumerate(ins)]
    park = pltpu.make_async_copy(moved_ref, q_far, sem.at[len(ins)])
    for copy in copies:
        copy.start()
    for i, copy in enumerate(copies):
        copy.wait()
        for h in range(kv_ref.shape[0]):
            piece = rows_ref[i, :, h * HEAD_DIM : (h + 1) * HEAD_DIM]
            if i == 0:
                moved_ref[h, 0] = piece
            else:
                kv_ref[h, i - 1] = piece
        if i == 0:
            park.start()
    park.wait()


def unpack_kernel(in_ref, out_ref, held_ref, sem):
    size = out_ref.shape[0] // PARTS
    copies = []
    for i in range(PARTS):
        rows = slice(i * size, (i + 1) * size)
        for h in range(in_ref.shape[0]):
            held_ref[rows, h * HEAD_DIM : (h + 1) * HEAD_DIM] = in_ref[h, rows]
        copies.append(pltpu.make_async_copy(held_ref.at[rows], out_ref.at[rows], sem.at[i]))
        copies[-1].start()
    for copy in copies:
        copy.wait()


def base_inverses(coupling):
    count, tiles, lanes = len(coupling), BLOCK // BASE, BLOCK
    tile = lax.broadcasted_iota(jnp.int32, (tiles, BASE, lanes), 0)
    lane = lax.broadcasted_iota(jnp.int32, (tiles, BASE, lanes), 2)
    own = lane // BASE == tile
    packed = [jnp.sum(jnp.where(own, n.reshape(tiles, BASE, lanes), 0.0), axis=0) for n in coupling]
    rows = split(jnp.concatenate(packed, axis=0))
    source = lax.broadcasted_iota(jnp.int32, (lanes, lanes), 0)
    target = lax.broadcasted_iota(jnp.int32, (lanes, lanes), 1)
    same = source // BASE == target // BASE
    spread = jnp.concatenate(
        [(same & (source % BASE == k)).astype(bf16) for k in range(BASE - 1)], axis=1
    )
    factors = mm(rows, twice(spread))
    sub = lax.broadcasted_iota(jnp.int32, (count, BASE, lanes), 1)
    at = lax.broadcasted_iota(jnp.int32, (count, BASE, lanes), 2) % BASE
    solved = (sub == at).astype(f32)
    for k in range(BASE - 1):
        factor = factors[:, k * lanes : (k + 1) * lanes].reshape(count, BASE, lanes)
        solved = solved - factor * solved[:, k : k + 1, :]
    return [
        jnp.where(own, jnp.broadcast_to(solved[i][None], (tiles, BASE, lanes)), 0.0).reshape(BLOCK, lanes)
        for i in range(count)
    ]


def maps_kernel(climb, kvq_ref, k_ref, w_ref, u_far, a_ref, b_ref, total_ref, u_ref, sem):
    count = kvq_ref.shape[0]
    park = pltpu.make_async_copy(u_ref, u_far, sem.at[0])
    offsets, _ = node_offsets(count)
    row, col = iotas()
    diagonal = row == col
    eye = diagonal.astype(f32)

    def run(blocks):
        keys = [kvq_ref[j, 0] for j in blocks]
        grams = [mm_nt(k, k) for k in keys]
        coupling, scale_cols, scale_rows = [], [], []
        for g in grams:
            on_diagonal = jnp.where(diagonal, g, 0.0)
            c = 1.0 / jnp.sqrt(jnp.sum(on_diagonal, axis=1, keepdims=True) + key_eps)
            r = 1.0 / jnp.sqrt(jnp.sum(on_diagonal, axis=0, keepdims=True) + key_eps)
            scale_cols.append(c)
            scale_rows.append(r)
            coupling.append(jnp.where(row > col, (2.0 * c) * g * r, 0.0))
        inverses = base_inverses(coupling)
        size = BASE
        while size < BLOCK:
            mask = ((row // size) % 2 == 1) & (col // size == row // size - 1)
            parts = [jnp.where(mask, n, 0.0) for n in coupling]
            pairs = [split(t) for t in inverses]
            inner = [product(split(p), t) for p, t in zip(parts, pairs)]
            outer = [product(t, split(z)) for t, z in zip(pairs, inner)]
            inverses = [t - z for t, z in zip(inverses, outer)]
            size *= 2
        lefts = [(2.0 * c) * t for c, t in zip(scale_cols, inverses)]
        weights = [split(mm(split(t * r), twice(k))) for t, r, k in zip(lefts, scale_rows, keys)]
        changes = [split(mm(split(t), twice(kvq_ref[j, 1]))) for t, j in zip(lefts, blocks)]
        for i, j in enumerate(blocks):
            u_ref[j] = changes[i]
        park.start()
        for i, j in enumerate(blocks):
            k_ref[j] = keys[i]
            w_ref[j] = weights[i]
            across = keys[i].T
            both = mm(jnp.concatenate([across, across], axis=1), stack(weights[i], changes[i]))
            a_ref[j] = split(eye - both[:, :HEAD_DIM])
            b_ref[j] = both[:, HEAD_DIM:]

    run(range(count))
    for level in range(1, len(offsets)):
        below, here = offsets[level - 1], offsets[level]
        for i in range(count >> level):
            first, second = below + 2 * i, below + 2 * i + 1
            later = a_ref[second]
            b_ref[here + i] = product(later, split(b_ref[first])) + b_ref[second]
            if climb or level < len(offsets) - 1:
                a_ref[here + i] = split(product(later, a_ref[first]))
    total_ref[...] = b_ref[offsets[-1]]
    park.wait()


def prefix_steps(count):
    offsets, _ = node_offsets(count)
    steps = []
    for level in range(len(offsets) - 2, -1, -1):
        here, above = offsets[level], offsets[level + 1]
        for i in range(count >> (level + 1)):
            parent = above + i if i > 0 else None
            if i > 0 or level == 0:
                steps.append((here + 2 * i, None, parent))
            steps.append((here + 2 * i + 1, here + 2 * i, parent))
    return steps


def sweep_kernel(a_ref, b_ref, pa_out, pb_out, pa_ref, pb_ref, sem):
    count = pa_out.shape[0]
    row, col = iotas()
    copies = []
    for (target, left, parent) in prefix_steps(count):
        if parent is None:
            pa_ref[target] = split((row == col).astype(f32)) if left is None else a_ref[left]
            pb_ref[target] = jnp.zeros((HEAD_DIM, HEAD_DIM), f32) if left is None else b_ref[left]
        elif left is None:
            pa_ref[target] = pa_ref[parent]
            pb_ref[target] = pb_ref[parent]
        else:
            pa_ref[target] = split(product(a_ref[left], pa_ref[parent]))
            pb_ref[target] = product(a_ref[left], split(pb_ref[parent])) + b_ref[left]
    leaves = pl.ds(0, count)
    copies = [
        pltpu.make_async_copy(pa_ref.at[leaves], pa_out, sem.at[0]),
        pltpu.make_async_copy(pb_ref.at[leaves], pb_out, sem.at[1]),
    ]
    for copy in copies:
        copy.start()
    for copy in copies:
        copy.wait()


def queries_kernel(q_ref, k_ref, w_ref, u_far, pa_far, pb_far, qp_ref, op_ref, u_ref, pa_ref, pb_ref, sem):
    count = k_ref.shape[0]
    row, col = iotas()
    causal = row >= col
    loads = [(u_far, u_ref), (pa_far, pa_ref), (pb_far, pb_ref)]
    copies = [pltpu.make_async_copy(source, target, sem.at[i]) for i, (source, target) in enumerate(loads)]
    for copy in copies:
        copy.start()
    blocks = range(count)
    scores = [split(jnp.where(causal, mm_nt(q_ref[j, 0], k_ref[j]), 0.0)) for j in blocks]
    through = [split(q_ref[j, 0].astype(f32) - product(c, w_ref[j])) for c, j in zip(scores, blocks)]
    copies[0].wait()
    local = [product(c, u_ref[j]) for c, j in zip(scores, blocks)]
    for copy in copies[1:]:
        copy.wait()
    joint = [product_wide(t, pa_ref[j], split(pb_ref[j])) for t, j in zip(through, blocks)]
    for j in blocks:
        qp_ref[j] = split(joint[j][:, :HEAD_DIM])
        op_ref[j] = joint[j][:, HEAD_DIM:] + local[j]


def finish_kernel(qp_ref, op_ref, state_ref, gain_ref, out_ref):
    arrived = jnp.where(lax.axis_index("hi") > 0, state_ref[...], 0.0)
    state = twice(split(arrived))
    gain = gain_ref[...]

    def run(blocks):
        outputs = [fold(mm(qp_ref[j], state)) + op_ref[j] for j in blocks]
        for j, output in zip(blocks, outputs):
            scale = lax.rsqrt(jnp.mean(output * output, axis=1, keepdims=True) + norm_eps)
            out_ref[j] = (output * scale * gain).astype(bf16)

    batches(out_ref.shape[0], run)


def call(kernel, name, outs, flops, kept=True, limit=24 << 20, scratch=(), in_space=None):
    spaces = [pltpu.VMEM if kept is True or i in (kept or ()) else pltpu.HBM for i in range(len(outs))]
    extra = {} if in_space is None else {"in_specs": [pl.BlockSpec(memory_space=s) for s in in_space]}
    return pl.pallas_call(
        kernel,
        name=name,
        out_shape=tuple(space(s, t) for space, (s, t) in zip(spaces, outs)),
        out_specs=tuple(pl.BlockSpec(memory_space=space) for space in spaces),
        scratch_shapes=list(scratch),
        compiler_params=pltpu.CompilerParams(vmem_limit_bytes=limit),
        cost_estimate=pl.CostEstimate(flops=flops, bytes_accessed=4 << 20, transcendentals=0),
        **extra,
    )


def held(space, *values):
    return [pltpu.with_memory_space_constraint(v, space) for v in values]


def near(*values):
    return held(pltpu.VMEM, *values)


def far(*values):
    return held(pltpu.HBM, *values)


def body(groups, lanes, queries, key_vectors, head_value_rows, out_gain):
    tokens, features = queries.shape
    if tokens != BLOCK or features != lanes * HEAD_DIM:
        raise ValueError("unsupported sizes")
    blocks = lanes
    _, nodes = node_offsets(blocks)
    one = (HEAD_DIM, HEAD_DIM)
    pair = (HEAD_DIM, 2 * HEAD_DIM)
    unit = 2 * BLOCK**3 * 4
    dma = pltpu.SemaphoreType.DMA

    kv_shape, q_shape = [(lanes, count, BLOCK, HEAD_DIM) for count in (2, 1)]
    kv, q = call(
        pack_kernel, "pack", [(kv_shape, bf16), (q_shape, bf16)], 0, kept=(0,),
        scratch=[pltpu.VMEM((3, tokens, features), bf16), pltpu.VMEM(q_shape, bf16), dma((4,))],
        in_space=[pltpu.HBM] * 3,
    )(*far(queries, key_vectors, head_value_rows))
    with jax.named_scope("kvmove"):
        kv = lax.all_to_all(kv, "lo", split_axis=0, concat_axis=0, tiled=True)
    with jax.named_scope("qmove"):
        q = lax.all_to_all(q, "lo", split_axis=0, concat_axis=0, tiled=True)
    with jax.named_scope("maps"):
        k, w, u, a, b, total = call(
            functools.partial(maps_kernel, groups > 2), "maps",
            [((blocks, *one), bf16), ((blocks, *pair), bf16), ((blocks, *pair), bf16),
             ((nodes, *pair), bf16), ((nodes, *one), f32), (one, f32)],
            unit * blocks * 20, kept=(0, 1, 3, 4, 5),
            scratch=[pltpu.VMEM((blocks, *pair), bf16), dma((1,))],
        )(*near(kv))
    hop = [(source, (source + 1) % groups) for source in range(groups)]
    with jax.named_scope("hop"):
        incoming = lax.ppermute(total, "hi", hop)
    if groups > 2:
        top = a[nodes - 1].astype(f32)
        transition = top[:, :HEAD_DIM] + top[:, HEAD_DIM:]

        def relay(i, arriving):
            arriving = jnp.where(lax.axis_index("hi") > 0, arriving, 0.0)
            leaving = jnp.dot(transition, arriving, precision=lax.Precision.HIGHEST) + total
            return lax.ppermute(leaving, "hi", hop)

        incoming = lax.fori_loop(0, groups - 2, relay, incoming)
    prefixes = [((blocks, *pair), bf16), ((blocks, *one), f32)]
    with jax.named_scope("sweep"):
        pa, pb = call(
            sweep_kernel, "sweep", prefixes, unit * blocks * 2, kept=False,
            scratch=[pltpu.VMEM((nodes, *pair), bf16), pltpu.VMEM((nodes, *one), f32), dma((2,))],
        )(*near(a, b))
    qp, op = call(
        queries_kernel, "queries", [((blocks, *pair), bf16), ((blocks, *one), f32)], unit * blocks * 6,
        scratch=[pltpu.VMEM((blocks, *pair), bf16)] + [pltpu.VMEM(s, t) for s, t in prefixes] + [dma((3,))],
        in_space=[pltpu.VMEM] * 3 + [pltpu.HBM] * 3,
    )(*near(q, k, w), *far(u, pa, pb))
    (out,) = call(
        finish_kernel, "finish", [((blocks, BLOCK, HEAD_DIM), bf16)], unit * blocks * 2,
    )(*near(qp, op), incoming, out_gain.reshape(1, HEAD_DIM))
    back = lax.all_to_all(out, "lo", split_axis=0, concat_axis=0, tiled=True)
    (mixed,) = call(
        unpack_kernel, "unpack", [((tokens, features), bf16)], 0, kept=False,
        scratch=[pltpu.VMEM((tokens, features), bf16), dma((PARTS,))],
    )(*near(back))
    return mixed


def solution(mesh):
    count = mesh.devices.size

    def run(queries, key_vectors, head_value_rows, out_gain):
        lanes = queries.shape[1] // HEAD_DIM
        regrouped = Mesh(mesh.devices.reshape(count // lanes, lanes), ("hi", "lo"))
        rows = P(("hi", "lo"), None)
        return jax.shard_map(
            functools.partial(body, count // lanes, lanes),
            mesh=regrouped, in_specs=(rows, rows, rows, P()), out_specs=rows, check_vma=False,
        )(queries, key_vectors, head_value_rows, out_gain)

    return run
```

```python
import functools

import jax
import jax.numpy as jnp
from jax import lax
from jax.experimental import pallas as pl
from jax.experimental.pallas import tpu as pltpu
from jax.sharding import Mesh
from jax.sharding import PartitionSpec as P

HEAD_DIM = 128
BLOCK = 128
key_eps = 1e-06
norm_eps = 1e-05
BATCH = 16
BASE = 16
PARTS = 4

f32 = jnp.float32
bf16 = jnp.bfloat16


def mm(left, right):
    return jnp.dot(left, right, preferred_element_type=f32)


def mm_nt(left, right):
    return lax.dot_general(left, right, (((1,), (1,)), ((), ())), preferred_element_type=f32)


def split(value):
    high = value.astype(bf16)
    low = (value - high.astype(f32)).astype(bf16)
    return jnp.concatenate([high, low], axis=1)


def twice(rows):
    return jnp.concatenate([rows, rows], axis=0)


def fold(wide):
    half = wide.shape[1] // 2
    return wide[:, :half] + wide[:, half:]


def stack(first_pair, second_pair):
    n = HEAD_DIM
    highs = jnp.concatenate([first_pair[:, :n], second_pair[:, :n]], axis=1)
    lows = jnp.concatenate([first_pair[:, n:], second_pair[:, n:]], axis=1)
    return jnp.concatenate([highs, lows], axis=0)


def product(left_pair, right_pair):
    return fold(mm(left_pair, twice(right_pair)))


def product_wide(left_pair, first_pair, second_pair):
    n = HEAD_DIM
    highs = jnp.concatenate([first_pair[:, :n], second_pair[:, :n]], axis=1)
    lows = jnp.concatenate([first_pair[:, n:], second_pair[:, n:]], axis=1)
    return mm(left_pair, twice(highs)) + mm(left_pair[:, :n], lows)


def iotas():
    row = lax.broadcasted_iota(jnp.int32, (BLOCK, BLOCK), 0)
    col = lax.broadcasted_iota(jnp.int32, (BLOCK, BLOCK), 1)
    return row, col


def batches(count, run):
    size = min(BATCH, count)
    if count == size:
        run([j for j in range(count)])
    else:
        def one(i, carried):
            run([i * size + j for j in range(size)])
            return carried
        lax.fori_loop(0, count // size, one, 0)


def node_offsets(count):
    offsets, at, size = [], 0, count
    while size >= 1:
        offsets.append(at)
        at += size
        size //= 2
    return offsets, at


def pack_kernel(*refs):
    *ins, out_ref, held_ref, sem = refs
    copies = [pltpu.make_async_copy(ref, held_ref.at[i], sem.at[i]) for i, ref in enumerate(ins)]
    for copy in copies:
        copy.start()
    for i, copy in enumerate(copies):
        copy.wait()
        for h in range(out_ref.shape[0]):
            out_ref[h, i] = held_ref[i, :, h * HEAD_DIM : (h + 1) * HEAD_DIM]


def base_inverses(coupling):
    count, tiles, lanes = len(coupling), BLOCK // BASE, BLOCK
    tile = lax.broadcasted_iota(jnp.int32, (tiles, BASE, lanes), 0)
    lane = lax.broadcasted_iota(jnp.int32, (tiles, BASE, lanes), 2)
    own = lane // BASE == tile
    packed = [jnp.sum(jnp.where(own, n.reshape(tiles, BASE, lanes), 0.0), axis=0) for n in coupling]
    rows = split(jnp.concatenate(packed, axis=0))
    source = lax.broadcasted_iota(jnp.int32, (lanes, lanes), 0)
    target = lax.broadcasted_iota(jnp.int32, (lanes, lanes), 1)
    same = source // BASE == target // BASE
    spread = jnp.concatenate(
        [(same & (source % BASE == k)).astype(bf16) for k in range(BASE - 1)], axis=1
    )
    factors = mm(rows, twice(spread))
    sub = lax.broadcasted_iota(jnp.int32, (count, BASE, lanes), 1)
    at = lax.broadcasted_iota(jnp.int32, (count, BASE, lanes), 2) % BASE
    solved = (sub == at).astype(f32)
    for k in range(BASE - 1):
        factor = factors[:, k * lanes : (k + 1) * lanes].reshape(count, BASE, lanes)
        solved = solved - factor * solved[:, k : k + 1, :]
    return [
        jnp.where(own, jnp.broadcast_to(solved[i][None], (tiles, BASE, lanes)), 0.0).reshape(BLOCK, lanes)
        for i in range(count)
    ]


def solve(keys, values):
    row, col = iotas()
    diagonal = row == col
    grams = [mm_nt(k, k) for k in keys]
    coupling, scale_cols, scale_rows = [], [], []
    for g in grams:
        on_diagonal = jnp.where(diagonal, g, 0.0)
        c = 1.0 / jnp.sqrt(jnp.sum(on_diagonal, axis=1, keepdims=True) + key_eps)
        r = 1.0 / jnp.sqrt(jnp.sum(on_diagonal, axis=0, keepdims=True) + key_eps)
        scale_cols.append(c)
        scale_rows.append(r)
        coupling.append(jnp.where(row > col, (2.0 * c) * g * r, 0.0))
    inverses = base_inverses(coupling)
    size = BASE
    while size < BLOCK:
        mask = ((row // size) % 2 == 1) & (col // size == row // size - 1)
        parts = [jnp.where(mask, n, 0.0) for n in coupling]
        pairs = [split(t) for t in inverses]
        inner = [product(split(p), t) for p, t in zip(parts, pairs)]
        outer = [product(t, split(z)) for t, z in zip(pairs, inner)]
        inverses = [t - z for t, z in zip(inverses, outer)]
        size *= 2
    lefts = [split((2.0 * c) * t) for c, t in zip(scale_cols, inverses)]
    units = [split(k.astype(f32) * c) for k, c in zip(keys, scale_cols)]
    firsts = [
        mm(t, twice(jnp.concatenate([k[:, :HEAD_DIM], v], axis=1)))
        for t, k, v in zip(lefts, units, values)
    ]
    rests = [mm(t[:, :HEAD_DIM], k[:, HEAD_DIM:]) for t, k in zip(lefts, units)]
    weights = [split(f[:, :HEAD_DIM] + r) for f, r in zip(firsts, rests)]
    changes = [split(f[:, HEAD_DIM:]) for f in firsts]
    return weights, changes


def maps_kernel(climb, kv_ref, a_ref, b_ref, total_ref):
    count = kv_ref.shape[0]
    offsets, _ = node_offsets(count)
    row, col = iotas()
    eye = (row == col).astype(f32)
    keys = [kv_ref[j, 0] for j in range(count)]
    weights, changes = solve(keys, [kv_ref[j, 1] for j in range(count)])
    for j in range(count):
        across = keys[j].T
        both = mm(jnp.concatenate([across, across], axis=1), stack(weights[j], changes[j]))
        a_ref[j] = split(eye - both[:, :HEAD_DIM])
        b_ref[j] = both[:, HEAD_DIM:]
    for level in range(1, len(offsets)):
        below, here = offsets[level - 1], offsets[level]
        for i in range(count >> level):
            first, second = below + 2 * i, below + 2 * i + 1
            later = a_ref[second]
            b_ref[here + i] = product(later, split(b_ref[first])) + b_ref[second]
            if climb or (i > 0 and level < len(offsets) - 1):
                a_ref[here + i] = split(product(later, a_ref[first]))
    total_ref[...] = b_ref[offsets[-1]]


def prefix_steps(count):
    offsets, _ = node_offsets(count)
    steps = []
    for level in range(len(offsets) - 2, -1, -1):
        here, above = offsets[level], offsets[level + 1]
        for i in range(count >> (level + 1)):
            parent = above + i if i > 0 else None
            if i > 0 or level == 0:
                steps.append((here + 2 * i, None, parent))
            steps.append((here + 2 * i + 1, here + 2 * i, parent))
    return steps


def sweep_kernel(a_ref, b_ref, pa_ref, pb_ref):
    count = (a_ref.shape[0] + 1) // 2
    row, col = iotas()
    offsets, _ = node_offsets(count)
    first = {0: a_ref[0]}
    for below, here in zip(offsets[:-2], offsets[1:-1]):
        first[here] = split(product(a_ref[below + 1], first[below]))
    for (target, left, parent) in prefix_steps(count):
        if parent is None:
            pa_ref[target] = split((row == col).astype(f32)) if left is None else first[left]
            pb_ref[target] = jnp.zeros((HEAD_DIM, HEAD_DIM), f32) if left is None else b_ref[left]
        elif left is None:
            pa_ref[target] = pa_ref[parent]
            pb_ref[target] = pb_ref[parent]
        else:
            pa_ref[target] = split(product(a_ref[left], pa_ref[parent]))
            pb_ref[target] = product(a_ref[left], split(pb_ref[parent])) + b_ref[left]


def states_kernel(pa_ref, pb_ref, state_ref, out_ref):
    arrived = jnp.where(lax.axis_index("hi") > 0, state_ref[...], 0.0)
    state = twice(split(arrived))
    for j in range(out_ref.shape[0]):
        out_ref[j] = (fold(mm(pa_ref[j], state)) + pb_ref[j]).astype(bf16)


def local_kernel(k_far, v_far, q_far, qt_ref, ol_ref, rows_ref, sem):
    heads = range(qt_ref.shape[0])
    sources = (k_far, v_far, q_far)
    copies = [pltpu.make_async_copy(ref, rows_ref.at[i], sem.at[i]) for i, ref in enumerate(sources)]
    for copy in copies:
        copy.start()
    for copy in copies:
        copy.wait()
    keys, values, asks = [
        [rows_ref[i, :, h * HEAD_DIM : (h + 1) * HEAD_DIM] for h in heads] for i in range(len(sources))
    ]
    weights, changes = solve(keys, values)
    row, col = iotas()
    causal = row >= col
    scores = [split(jnp.where(causal, mm_nt(q, k), 0.0)) for q, k in zip(asks, keys)]
    for h in heads:
        joint = product_wide(scores[h], weights[h], changes[h])
        qt_ref[h] = split(asks[h].astype(f32) - joint[:, :HEAD_DIM])
        ol_ref[h] = joint[:, HEAD_DIM:]


def final_kernel(qt_ref, ol_ref, state_ref, gain_ref, out_far, rows_ref, sem):
    heads = qt_ref.shape[0]
    gain = gain_ref[...]
    width = heads // PARTS * HEAD_DIM
    copies = []
    for h in range(heads):
        output = mm(qt_ref[h], twice(state_ref[h])) + ol_ref[h]
        scale = lax.rsqrt(jnp.mean(output * output, axis=1, keepdims=True) + norm_eps)
        rows_ref[:, h * HEAD_DIM : (h + 1) * HEAD_DIM] = (output * scale * gain).astype(bf16)
        if (h + 1) % (heads // PARTS) == 0:
            i = h // (heads // PARTS)
            part = pl.ds(i * width, width)
            copies.append(pltpu.make_async_copy(rows_ref.at[:, part], out_far.at[:, part], sem.at[i]))
            copies[-1].start()
    for copy in copies:
        copy.wait()


def call(kernel, name, outs, flops, kept=True, limit=24 << 20, scratch=(), in_space=None):
    vmem = pl.BlockSpec(memory_space=pltpu.VMEM)
    far = pl.BlockSpec(memory_space=pltpu.HBM)
    make = pltpu.VMEM if kept else jax.ShapeDtypeStruct
    extra = {} if in_space is None else {"in_specs": [pl.BlockSpec(memory_space=s) for s in in_space]}
    return pl.pallas_call(
        kernel,
        name=name,
        out_shape=tuple(make(s, t) for s, t in outs),
        out_specs=tuple(vmem if kept else far for _ in outs),
        scratch_shapes=list(scratch),
        compiler_params=pltpu.CompilerParams(vmem_limit_bytes=limit),
        cost_estimate=pl.CostEstimate(flops=flops, bytes_accessed=4 << 20, transcendentals=0),
        **extra,
    )


def held(space, *values):
    return [pltpu.with_memory_space_constraint(v, space) for v in values]


def near(*values):
    return held(pltpu.VMEM, *values)


def body(groups, lanes, queries, key_vectors, head_value_rows, out_gain):
    tokens, features = queries.shape
    if tokens != BLOCK or features != lanes * HEAD_DIM:
        raise ValueError("unsupported sizes")
    blocks = lanes
    _, nodes = node_offsets(blocks)
    one = (HEAD_DIM, HEAD_DIM)
    pair = (HEAD_DIM, 2 * HEAD_DIM)
    unit = 2 * BLOCK**3 * 4
    dma = pltpu.SemaphoreType.DMA
    (pieces,) = call(
        pack_kernel, "pack", [((lanes, 2, BLOCK, HEAD_DIM), bf16)], 0,
        scratch=[pltpu.VMEM((2, tokens, features), bf16), dma((2,))], in_space=[pltpu.HBM] * 2,
    )(*held(pltpu.HBM, key_vectors, head_value_rows))
    kv = lax.all_to_all(pieces, "lo", split_axis=0, concat_axis=0, tiled=True)
    a, b, total = call(
        functools.partial(maps_kernel, groups > 2), "maps",
        [((nodes, *pair), bf16), ((nodes, *one), f32), (one, f32)], unit * blocks * 20,
    )(*near(kv))
    hop = [(source, (source + 1) % groups) for source in range(groups)]
    incoming = lax.ppermute(total, "hi", hop)
    if groups > 2:
        top = a[nodes - 1].astype(f32)
        transition = top[:, :HEAD_DIM] + top[:, HEAD_DIM:]

        def relay(i, arriving):
            arriving = jnp.where(lax.axis_index("hi") > 0, arriving, 0.0)
            leaving = jnp.dot(transition, arriving, precision=lax.Precision.HIGHEST) + total
            return lax.ppermute(leaving, "hi", hop)

        incoming = lax.fori_loop(0, groups - 2, relay, incoming)
    pa, pb = call(
        sweep_kernel, "sweep", [((nodes, *pair), bf16), ((nodes, *one), f32)], unit * blocks * 2,
    )(*near(a, b))
    (states,) = call(
        states_kernel, "states", [((blocks, *one), bf16)], unit * blocks,
    )(*near(pa, pb), incoming)
    states, queries, key_vectors, head_value_rows = lax.optimization_barrier(
        (states, queries, key_vectors, head_value_rows)
    )
    back = lax.all_to_all(states, "lo", split_axis=0, concat_axis=0, tiled=True)
    qt, ol = call(
        local_kernel, "local", [((lanes, *pair), bf16), ((lanes, *one), f32)], unit * blocks * 20,
        scratch=[pltpu.VMEM((3, tokens, features), bf16), dma((3,))], in_space=[pltpu.HBM] * 3,
    )(*held(pltpu.HBM, key_vectors, head_value_rows, queries))
    (mixed,) = call(
        final_kernel, "final", [((tokens, features), bf16)], unit * blocks, kept=False,
        scratch=[pltpu.VMEM((tokens, features), bf16), dma((PARTS,))],
    )(*near(qt, ol, back), out_gain.reshape(1, HEAD_DIM))
    return mixed


def solution(mesh):
    count = mesh.devices.size

    def run(queries, key_vectors, head_value_rows, out_gain):
        lanes = queries.shape[1] // HEAD_DIM
        regrouped = Mesh(mesh.devices.reshape(count // lanes, lanes), ("hi", "lo"))
        rows = P(("hi", "lo"), None)
        return jax.shard_map(
            functools.partial(body, count // lanes, lanes),
            mesh=regrouped, in_specs=(rows, rows, rows, P()), out_specs=rows, check_vma=False,
        )(queries, key_vectors, head_value_rows, out_gain)

    return run
```

```python
import functools

import jax
import jax.numpy as jnp
from jax import lax
from jax.experimental import pallas as pl
from jax.experimental.pallas import tpu as pltpu
from jax.sharding import Mesh
from jax.sharding import PartitionSpec as P

HEAD_DIM = 128
BLOCK = 128
key_eps = 1e-06
norm_eps = 1e-05
BATCH = 16
BASE = 16
PARTS = 4

f32 = jnp.float32
bf16 = jnp.bfloat16


def mm(left, right):
    return jnp.dot(left, right, preferred_element_type=f32)


def mm_nt(left, right):
    return lax.dot_general(left, right, (((1,), (1,)), ((), ())), preferred_element_type=f32)


def split(value):
    high = value.astype(bf16)
    low = (value - high.astype(f32)).astype(bf16)
    return jnp.concatenate([high, low], axis=1)


def twice(rows):
    return jnp.concatenate([rows, rows], axis=0)


def fold(wide):
    half = wide.shape[1] // 2
    return wide[:, :half] + wide[:, half:]


def stack(first_pair, second_pair):
    n = HEAD_DIM
    highs = jnp.concatenate([first_pair[:, :n], second_pair[:, :n]], axis=1)
    lows = jnp.concatenate([first_pair[:, n:], second_pair[:, n:]], axis=1)
    return jnp.concatenate([highs, lows], axis=0)


def product(left_pair, right_pair):
    return fold(mm(left_pair, twice(right_pair)))


def product_wide(left_pair, first_pair, second_pair):
    n = HEAD_DIM
    highs = jnp.concatenate([first_pair[:, :n], second_pair[:, :n]], axis=1)
    lows = jnp.concatenate([first_pair[:, n:], second_pair[:, n:]], axis=1)
    return mm(left_pair, twice(highs)) + mm(left_pair[:, :n], lows)


def iotas():
    row = lax.broadcasted_iota(jnp.int32, (BLOCK, BLOCK), 0)
    col = lax.broadcasted_iota(jnp.int32, (BLOCK, BLOCK), 1)
    return row, col


def batches(count, run):
    size = min(BATCH, count)
    if count == size:
        run([j for j in range(count)])
    else:
        def one(i, carried):
            run([i * size + j for j in range(size)])
            return carried
        lax.fori_loop(0, count // size, one, 0)


def node_offsets(count):
    offsets, at, size = [], 0, count
    while size >= 1:
        offsets.append(at)
        at += size
        size //= 2
    return offsets, at


def pack_kernel(*refs):
    *ins, out_ref, held_ref, sem = refs
    copies = [pltpu.make_async_copy(ref, held_ref.at[i], sem.at[i]) for i, ref in enumerate(ins)]
    for copy in copies:
        copy.start()
    for i, copy in enumerate(copies):
        copy.wait()
        for h in range(out_ref.shape[0]):
            out_ref[h, i] = held_ref[i, :, h * HEAD_DIM : (h + 1) * HEAD_DIM]


def base_inverses(coupling):
    count, tiles, lanes = len(coupling), BLOCK // BASE, BLOCK
    tile = lax.broadcasted_iota(jnp.int32, (tiles, BASE, lanes), 0)
    lane = lax.broadcasted_iota(jnp.int32, (tiles, BASE, lanes), 2)
    own = lane // BASE == tile
    packed = [jnp.sum(jnp.where(own, n.reshape(tiles, BASE, lanes), 0.0), axis=0) for n in coupling]
    rows = split(jnp.concatenate(packed, axis=0))
    source = lax.broadcasted_iota(jnp.int32, (lanes, lanes), 0)
    target = lax.broadcasted_iota(jnp.int32, (lanes, lanes), 1)
    same = source // BASE == target // BASE
    spread = jnp.concatenate(
        [(same & (source % BASE == k)).astype(bf16) for k in range(BASE - 1)], axis=1
    )
    factors = mm(rows, twice(spread))
    sub = lax.broadcasted_iota(jnp.int32, (count, BASE, lanes), 1)
    at = lax.broadcasted_iota(jnp.int32, (count, BASE, lanes), 2) % BASE
    solved = (sub == at).astype(f32)
    for k in range(BASE - 1):
        factor = factors[:, k * lanes : (k + 1) * lanes].reshape(count, BASE, lanes)
        solved = solved - factor * solved[:, k : k + 1, :]
    return [
        jnp.where(own, jnp.broadcast_to(solved[i][None], (tiles, BASE, lanes)), 0.0).reshape(BLOCK, lanes)
        for i in range(count)
    ]


def solve(keys, values):
    row, col = iotas()
    diagonal = row == col
    grams = [mm_nt(k, k) for k in keys]
    coupling, scale_cols, scale_rows = [], [], []
    for g in grams:
        on_diagonal = jnp.where(diagonal, g, 0.0)
        c = 1.0 / jnp.sqrt(jnp.sum(on_diagonal, axis=1, keepdims=True) + key_eps)
        r = 1.0 / jnp.sqrt(jnp.sum(on_diagonal, axis=0, keepdims=True) + key_eps)
        scale_cols.append(c)
        scale_rows.append(r)
        coupling.append(jnp.where(row > col, (2.0 * c) * g * r, 0.0))
    inverses = base_inverses(coupling)
    size = BASE
    while size < BLOCK:
        mask = ((row // size) % 2 == 1) & (col // size == row // size - 1)
        parts = [jnp.where(mask, n, 0.0) for n in coupling]
        pairs = [split(t) for t in inverses]
        inner = [product(split(p), t) for p, t in zip(parts, pairs)]
        outer = [product(t, split(z)) for t, z in zip(pairs, inner)]
        inverses = [t - z for t, z in zip(inverses, outer)]
        size *= 2
    lefts = [split((2.0 * c) * t) for c, t in zip(scale_cols, inverses)]
    units = [split(k.astype(f32) * c) for k, c in zip(keys, scale_cols)]
    firsts = [
        mm(t, twice(jnp.concatenate([k[:, :HEAD_DIM], v], axis=1)))
        for t, k, v in zip(lefts, units, values)
    ]
    rests = [mm(t[:, :HEAD_DIM], k[:, HEAD_DIM:]) for t, k in zip(lefts, units)]
    weights = [split(f[:, :HEAD_DIM] + r) for f, r in zip(firsts, rests)]
    changes = [split(f[:, HEAD_DIM:]) for f in firsts]
    return weights, changes


def maps_kernel(climb, kv_ref, a_ref, b_ref, total_ref):
    count = kv_ref.shape[0]
    offsets, _ = node_offsets(count)
    row, col = iotas()
    eye = (row == col).astype(f32)
    keys = [kv_ref[j, 0] for j in range(count)]
    weights, changes = solve(keys, [kv_ref[j, 1] for j in range(count)])
    for j in range(count):
        across = keys[j].T
        both = mm(jnp.concatenate([across, across], axis=1), stack(weights[j], changes[j]))
        a_ref[j] = split(eye - both[:, :HEAD_DIM])
        b_ref[j] = both[:, HEAD_DIM:]
    for level in range(1, len(offsets)):
        below, here = offsets[level - 1], offsets[level]
        for i in range(count >> level):
            first, second = below + 2 * i, below + 2 * i + 1
            later = a_ref[second]
            b_ref[here + i] = product(later, split(b_ref[first])) + b_ref[second]
            if climb or (i > 0 and level < len(offsets) - 1):
                a_ref[here + i] = split(product(later, a_ref[first]))
    total_ref[...] = b_ref[offsets[-1]].astype(total_ref.dtype)


def prefix_steps(count):
    offsets, _ = node_offsets(count)
    steps = []
    for level in range(len(offsets) - 2, -1, -1):
        here, above = offsets[level], offsets[level + 1]
        for i in range(count >> (level + 1)):
            parent = above + i if i > 0 else None
            if i > 0 or level == 0:
                steps.append((here + 2 * i, None, parent))
            steps.append((here + 2 * i + 1, here + 2 * i, parent))
    return steps


def sweep_kernel(a_ref, b_ref, pa_ref, pb_ref):
    count = (a_ref.shape[0] + 1) // 2
    row, col = iotas()
    offsets, _ = node_offsets(count)
    first = {0: a_ref[0]}
    for below, here in zip(offsets[:-2], offsets[1:-1]):
        first[here] = split(product(a_ref[below + 1], first[below]))
    for (target, left, parent) in prefix_steps(count):
        if parent is None:
            pa_ref[target] = split((row == col).astype(f32)) if left is None else first[left]
            pb_ref[target] = jnp.zeros((HEAD_DIM, HEAD_DIM), f32) if left is None else b_ref[left]
        elif left is None:
            pa_ref[target] = pa_ref[parent]
            pb_ref[target] = pb_ref[parent]
        else:
            pa_ref[target] = split(product(a_ref[left], pa_ref[parent]))
            pb_ref[target] = product(a_ref[left], split(pb_ref[parent])) + b_ref[left]


def states_kernel(pa_ref, pb_ref, state_ref, out_ref):
    arrived = jnp.where(lax.axis_index("hi") > 0, state_ref[...].astype(f32), 0.0)
    state = twice(split(arrived))
    for j in range(out_ref.shape[0]):
        out_ref[j] = (fold(mm(pa_ref[j], state)) + pb_ref[j]).astype(bf16)


def local_kernel(k_far, v_far, q_far, qt_ref, ol_ref, rows_ref, sem):
    heads = range(qt_ref.shape[0])
    sources = (k_far, v_far, q_far)
    copies = [pltpu.make_async_copy(ref, rows_ref.at[i], sem.at[i]) for i, ref in enumerate(sources)]
    for copy in copies:
        copy.start()
    for copy in copies:
        copy.wait()
    keys, values, asks = [
        [rows_ref[i, :, h * HEAD_DIM : (h + 1) * HEAD_DIM] for h in heads] for i in range(len(sources))
    ]
    weights, changes = solve(keys, values)
    row, col = iotas()
    causal = row >= col
    scores = [split(jnp.where(causal, mm_nt(q, k), 0.0)) for q, k in zip(asks, keys)]
    for h in heads:
        joint = product_wide(scores[h], weights[h], changes[h])
        qt_ref[h] = split(asks[h].astype(f32) - joint[:, :HEAD_DIM])
        ol_ref[h] = joint[:, HEAD_DIM:]


def final_kernel(qt_ref, ol_ref, state_ref, gain_ref, out_far, rows_ref, sem):
    heads = qt_ref.shape[0]
    gain = gain_ref[...]
    width = heads // PARTS * HEAD_DIM
    copies = []
    for h in range(heads):
        output = mm(qt_ref[h], twice(state_ref[h])) + ol_ref[h]
        scale = lax.rsqrt(jnp.mean(output * output, axis=1, keepdims=True) + norm_eps)
        rows_ref[:, h * HEAD_DIM : (h + 1) * HEAD_DIM] = (output * scale * gain).astype(bf16)
        if (h + 1) % (heads // PARTS) == 0:
            i = h // (heads // PARTS)
            part = pl.ds(i * width, width)
            copies.append(pltpu.make_async_copy(rows_ref.at[:, part], out_far.at[:, part], sem.at[i]))
            copies[-1].start()
    for copy in copies:
        copy.wait()


def call(kernel, name, outs, flops, kept=True, limit=24 << 20, scratch=(), in_space=None):
    vmem = pl.BlockSpec(memory_space=pltpu.VMEM)
    far = pl.BlockSpec(memory_space=pltpu.HBM)
    make = pltpu.VMEM if kept else jax.ShapeDtypeStruct
    extra = {} if in_space is None else {"in_specs": [pl.BlockSpec(memory_space=s) for s in in_space]}
    return pl.pallas_call(
        kernel,
        name=name,
        out_shape=tuple(make(s, t) for s, t in outs),
        out_specs=tuple(vmem if kept else far for _ in outs),
        scratch_shapes=list(scratch),
        compiler_params=pltpu.CompilerParams(vmem_limit_bytes=limit),
        cost_estimate=pl.CostEstimate(flops=flops, bytes_accessed=4 << 20, transcendentals=0),
        **extra,
    )


def held(space, *values):
    return [pltpu.with_memory_space_constraint(v, space) for v in values]


def near(*values):
    return held(pltpu.VMEM, *values)


def body(groups, lanes, queries, key_vectors, head_value_rows, out_gain):
    tokens, features = queries.shape
    if tokens != BLOCK or features != lanes * HEAD_DIM:
        raise ValueError("unsupported sizes")
    blocks = lanes
    _, nodes = node_offsets(blocks)
    one = (HEAD_DIM, HEAD_DIM)
    pair = (HEAD_DIM, 2 * HEAD_DIM)
    unit = 2 * BLOCK**3 * 4
    dma = pltpu.SemaphoreType.DMA
    (pieces,) = call(
        pack_kernel, "pack", [((lanes, 2, BLOCK, HEAD_DIM), bf16)], 0,
        scratch=[pltpu.VMEM((2, tokens, features), bf16), dma((2,))], in_space=[pltpu.HBM] * 2,
    )(*held(pltpu.HBM, key_vectors, head_value_rows))
    kv = lax.all_to_all(pieces, "lo", split_axis=0, concat_axis=0, tiled=True)
    a, b, total = call(
        functools.partial(maps_kernel, groups > 2), "maps",
        [((nodes, *pair), bf16), ((nodes, *one), f32), (one, bf16 if groups == 2 else f32)], unit * blocks * 20,
    )(*near(kv))
    hop = [(source, (source + 1) % groups) for source in range(groups)]
    incoming = lax.ppermute(total, "hi", hop)
    if groups > 2:
        top = a[nodes - 1].astype(f32)
        transition = top[:, :HEAD_DIM] + top[:, HEAD_DIM:]

        def relay(i, arriving):
            arriving = jnp.where(lax.axis_index("hi") > 0, arriving, 0.0)
            leaving = jnp.dot(transition, arriving, precision=lax.Precision.HIGHEST) + total
            return lax.ppermute(leaving, "hi", hop)

        incoming = lax.fori_loop(0, groups - 2, relay, incoming)
    pa, pb = call(
        sweep_kernel, "sweep", [((nodes, *pair), bf16), ((nodes, *one), f32)], unit * blocks * 2,
    )(*near(a, b))
    (states,) = call(
        states_kernel, "states", [((blocks, *one), bf16)], unit * blocks,
    )(*near(pa, pb), incoming)
    states, queries, key_vectors, head_value_rows = lax.optimization_barrier(
        (states, queries, key_vectors, head_value_rows)
    )
    back = lax.all_to_all(states, "lo", split_axis=0, concat_axis=0, tiled=True)
    qt, ol = call(
        local_kernel, "local", [((lanes, *pair), bf16), ((lanes, *one), f32)], unit * blocks * 20,
        scratch=[pltpu.VMEM((3, tokens, features), bf16), dma((3,))], in_space=[pltpu.HBM] * 3,
    )(*held(pltpu.HBM, key_vectors, head_value_rows, queries))
    (mixed,) = call(
        final_kernel, "final", [((tokens, features), bf16)], unit * blocks, kept=False,
        scratch=[pltpu.VMEM((tokens, features), bf16), dma((PARTS,))],
    )(*near(qt, ol, back), out_gain.reshape(1, HEAD_DIM))
    return mixed


def solution(mesh):
    count = mesh.devices.size

    def run(queries, key_vectors, head_value_rows, out_gain):
        lanes = queries.shape[1] // HEAD_DIM
        regrouped = Mesh(mesh.devices.reshape(count // lanes, lanes), ("hi", "lo"))
        rows = P(("hi", "lo"), None)
        return jax.shard_map(
            functools.partial(body, count // lanes, lanes),
            mesh=regrouped, in_specs=(rows, rows, rows, P()), out_specs=rows, check_vma=False,
        )(queries, key_vectors, head_value_rows, out_gain)

    return run
```

```python
import functools

import jax
import jax.numpy as jnp
from jax import lax
from jax.experimental import pallas as pl
from jax.experimental.pallas import tpu as pltpu
from jax.sharding import Mesh
from jax.sharding import PartitionSpec as P

HEAD_DIM = 128
BLOCK = 128
key_eps = 1e-06
norm_eps = 1e-05
BATCH = 16
BASE = 16
PARTS = 4

f32 = jnp.float32
bf16 = jnp.bfloat16


def mm(left, right):
    return jnp.dot(left, right, preferred_element_type=f32)


def mm_nt(left, right):
    return lax.dot_general(left, right, (((1,), (1,)), ((), ())), preferred_element_type=f32)


def split(value):
    high = value.astype(bf16)
    low = (value - high.astype(f32)).astype(bf16)
    return jnp.concatenate([high, low], axis=1)


def twice(rows):
    return jnp.concatenate([rows, rows], axis=0)


def fold(wide):
    half = wide.shape[1] // 2
    return wide[:, :half] + wide[:, half:]


def stack(first_pair, second_pair):
    n = HEAD_DIM
    highs = jnp.concatenate([first_pair[:, :n], second_pair[:, :n]], axis=1)
    lows = jnp.concatenate([first_pair[:, n:], second_pair[:, n:]], axis=1)
    return jnp.concatenate([highs, lows], axis=0)


def product(left_pair, right_pair):
    return fold(mm(left_pair, twice(right_pair)))


def product_wide(left_pair, first_pair, second_pair):
    n = HEAD_DIM
    highs = jnp.concatenate([first_pair[:, :n], second_pair[:, :n]], axis=1)
    lows = jnp.concatenate([first_pair[:, n:], second_pair[:, n:]], axis=1)
    return mm(left_pair, twice(highs)) + mm(left_pair[:, :n], lows)


def iotas():
    row = lax.broadcasted_iota(jnp.int32, (BLOCK, BLOCK), 0)
    col = lax.broadcasted_iota(jnp.int32, (BLOCK, BLOCK), 1)
    return row, col


def batches(count, run):
    size = min(BATCH, count)
    if count == size:
        run([j for j in range(count)])
    else:
        def one(i, carried):
            run([i * size + j for j in range(size)])
            return carried
        lax.fori_loop(0, count // size, one, 0)


def node_offsets(count):
    offsets, at, size = [], 0, count
    while size >= 1:
        offsets.append(at)
        at += size
        size //= 2
    return offsets, at


def pack_kernel(*refs):
    *ins, out_ref, held_ref, sem = refs
    copies = [pltpu.make_async_copy(ref, held_ref.at[i], sem.at[i]) for i, ref in enumerate(ins)]
    for copy in copies:
        copy.start()
    for i, copy in enumerate(copies):
        copy.wait()
        for h in range(out_ref.shape[0]):
            out_ref[h, i] = held_ref[i, :, h * HEAD_DIM : (h + 1) * HEAD_DIM]


def base_inverses(coupling):
    count, tiles, lanes = len(coupling), BLOCK // BASE, BLOCK
    tile = lax.broadcasted_iota(jnp.int32, (tiles, BASE, lanes), 0)
    lane = lax.broadcasted_iota(jnp.int32, (tiles, BASE, lanes), 2)
    own = lane // BASE == tile
    packed = [jnp.sum(jnp.where(own, n.reshape(tiles, BASE, lanes), 0.0), axis=0) for n in coupling]
    rows = split(jnp.concatenate(packed, axis=0))
    source = lax.broadcasted_iota(jnp.int32, (lanes, lanes), 0)
    target = lax.broadcasted_iota(jnp.int32, (lanes, lanes), 1)
    same = source // BASE == target // BASE
    spread = jnp.concatenate(
        [(same & (source % BASE == k)).astype(bf16) for k in range(BASE - 1)], axis=1
    )
    factors = mm(rows, twice(spread))
    sub = lax.broadcasted_iota(jnp.int32, (count, BASE, lanes), 1)
    at = lax.broadcasted_iota(jnp.int32, (count, BASE, lanes), 2) % BASE
    solved = (sub == at).astype(f32)
    for k in range(BASE - 1):
        factor = factors[:, k * lanes : (k + 1) * lanes].reshape(count, BASE, lanes)
        solved = solved - factor * solved[:, k : k + 1, :]
    return [
        jnp.where(own, jnp.broadcast_to(solved[i][None], (tiles, BASE, lanes)), 0.0).reshape(BLOCK, lanes)
        for i in range(count)
    ]


def solve(keys, values):
    row, col = iotas()
    diagonal = row == col
    grams = [mm_nt(k, k) for k in keys]
    coupling, scale_cols, scale_rows = [], [], []
    for g in grams:
        on_diagonal = jnp.where(diagonal, g, 0.0)
        c = 1.0 / jnp.sqrt(jnp.sum(on_diagonal, axis=1, keepdims=True) + key_eps)
        r = 1.0 / jnp.sqrt(jnp.sum(on_diagonal, axis=0, keepdims=True) + key_eps)
        scale_cols.append(c)
        scale_rows.append(r)
        coupling.append(jnp.where(row > col, (2.0 * c) * g * r, 0.0))
    inverses = base_inverses(coupling)
    size = BASE
    while size < BLOCK:
        mask = ((row // size) % 2 == 1) & (col // size == row // size - 1)
        parts = [jnp.where(mask, n, 0.0) for n in coupling]
        pairs = [split(t) for t in inverses]
        inner = [product(split(p), t) for p, t in zip(parts, pairs)]
        outer = [product(t, split(z)) for t, z in zip(pairs, inner)]
        inverses = [t - z for t, z in zip(inverses, outer)]
        size *= 2
    lefts = [split((2.0 * c) * t) for c, t in zip(scale_cols, inverses)]
    units = [split(k.astype(f32) * c) for k, c in zip(keys, scale_cols)]
    firsts = [
        mm(t, twice(jnp.concatenate([k[:, :HEAD_DIM], v], axis=1)))
        for t, k, v in zip(lefts, units, values)
    ]
    rests = [mm(t[:, :HEAD_DIM], k[:, HEAD_DIM:]) for t, k in zip(lefts, units)]
    weights = [split(f[:, :HEAD_DIM] + r) for f, r in zip(firsts, rests)]
    changes = [split(f[:, HEAD_DIM:]) for f in firsts]
    return weights, changes


def maps_kernel(climb, kv_ref, a_ref, b_ref, total_ref):
    count = kv_ref.shape[0]
    offsets, _ = node_offsets(count)
    row, col = iotas()
    eye = (row == col).astype(f32)
    keys = [kv_ref[j, 0] for j in range(count)]
    weights, changes = solve(keys, [kv_ref[j, 1] for j in range(count)])
    for j in range(count):
        across = keys[j].T
        both = mm(jnp.concatenate([across, across], axis=1), stack(weights[j], changes[j]))
        a_ref[j] = split(eye - both[:, :HEAD_DIM])
        b_ref[j] = both[:, HEAD_DIM:]
    for level in range(1, len(offsets)):
        below, here = offsets[level - 1], offsets[level]
        for i in range(count >> level):
            first, second = below + 2 * i, below + 2 * i + 1
            later = a_ref[second]
            b_ref[here + i] = product(later, split(b_ref[first])) + b_ref[second]
            if climb or (i > 0 and level < len(offsets) - 1):
                a_ref[here + i] = split(product(later, a_ref[first]))
    total_ref[...] = b_ref[offsets[-1]].astype(total_ref.dtype)


def prefix_steps(count):
    offsets, _ = node_offsets(count)
    steps = []
    for level in range(len(offsets) - 2, -1, -1):
        here, above = offsets[level], offsets[level + 1]
        for i in range(count >> (level + 1)):
            parent = above + i if i > 0 else None
            if i > 0 or level == 0:
                steps.append((here + 2 * i, None, parent))
            steps.append((here + 2 * i + 1, here + 2 * i, parent))
    return steps


def sweep_kernel(a_ref, b_ref, pa_ref, pb_ref):
    count = (a_ref.shape[0] + 1) // 2
    row, col = iotas()
    offsets, _ = node_offsets(count)
    first = {0: a_ref[0]}
    for below, here in zip(offsets[:-2], offsets[1:-1]):
        first[here] = split(product(a_ref[below + 1], first[below]))
    for (target, left, parent) in prefix_steps(count):
        if parent is None:
            pa_ref[target] = split((row == col).astype(f32)) if left is None else first[left]
            pb_ref[target] = jnp.zeros((HEAD_DIM, HEAD_DIM), f32) if left is None else b_ref[left]
        elif left is None:
            pa_ref[target] = pa_ref[parent]
            pb_ref[target] = pb_ref[parent]
        else:
            pa_ref[target] = split(product(a_ref[left], pa_ref[parent]))
            pb_ref[target] = product(a_ref[left], split(pb_ref[parent])) + b_ref[left]


def states_kernel(pa_ref, pb_ref, state_ref, out_far, rows_ref, sem):
    arrived = jnp.where(lax.axis_index("hi") > 0, state_ref[...].astype(f32), 0.0)
    exact = state_ref.dtype == bf16
    state = twice(arrived.astype(bf16) if exact else split(arrived))
    count = rows_ref.shape[0]
    size = count // PARTS
    copies = []
    for j in range(count):
        moved = mm(pa_ref[j], state)
        rows_ref[j] = ((moved if exact else fold(moved)) + pb_ref[j]).astype(bf16)
        if (j + 1) % size == 0:
            part = pl.ds(j + 1 - size, size)
            copies.append(pltpu.make_async_copy(rows_ref.at[part], out_far.at[part], sem.at[len(copies)]))
            copies[-1].start()
    for copy in copies:
        copy.wait()


def local_kernel(k_far, v_far, q_far, qt_ref, ol_ref, rows_ref, sem):
    heads = range(qt_ref.shape[0])
    sources = (k_far, v_far, q_far)
    copies = [pltpu.make_async_copy(ref, rows_ref.at[i], sem.at[i]) for i, ref in enumerate(sources)]
    for copy in copies:
        copy.start()
    for copy in copies:
        copy.wait()
    keys, values, asks = [
        [rows_ref[i, :, h * HEAD_DIM : (h + 1) * HEAD_DIM] for h in heads] for i in range(len(sources))
    ]
    weights, changes = solve(keys, values)
    row, col = iotas()
    causal = row >= col
    scores = [split(jnp.where(causal, mm_nt(q, k), 0.0)) for q, k in zip(asks, keys)]
    for h in heads:
        joint = product_wide(scores[h], weights[h], changes[h])
        qt_ref[h] = split(asks[h].astype(f32) - joint[:, :HEAD_DIM])
        ol_ref[h] = joint[:, HEAD_DIM:]


def final_kernel(qt_ref, ol_ref, state_ref, gain_ref, out_far, rows_ref, sem):
    heads = qt_ref.shape[0]
    gain = gain_ref[...]
    width = heads // PARTS * HEAD_DIM
    copies = []
    for h in range(heads):
        output = mm(qt_ref[h], twice(state_ref[h])) + ol_ref[h]
        scale = lax.rsqrt(jnp.mean(output * output, axis=1, keepdims=True) + norm_eps)
        rows_ref[:, h * HEAD_DIM : (h + 1) * HEAD_DIM] = (output * scale * gain).astype(bf16)
        if (h + 1) % (heads // PARTS) == 0:
            i = h // (heads // PARTS)
            part = pl.ds(i * width, width)
            copies.append(pltpu.make_async_copy(rows_ref.at[:, part], out_far.at[:, part], sem.at[i]))
            copies[-1].start()
    for copy in copies:
        copy.wait()


def call(kernel, name, outs, flops, kept=True, limit=24 << 20, scratch=(), in_space=None):
    vmem = pl.BlockSpec(memory_space=pltpu.VMEM)
    far = pl.BlockSpec(memory_space=pltpu.HBM)
    make = pltpu.VMEM if kept else jax.ShapeDtypeStruct
    extra = {} if in_space is None else {"in_specs": [pl.BlockSpec(memory_space=s) for s in in_space]}
    return pl.pallas_call(
        kernel,
        name=name,
        out_shape=tuple(make(s, t) for s, t in outs),
        out_specs=tuple(vmem if kept else far for _ in outs),
        scratch_shapes=list(scratch),
        compiler_params=pltpu.CompilerParams(vmem_limit_bytes=limit),
        cost_estimate=pl.CostEstimate(flops=flops, bytes_accessed=4 << 20, transcendentals=0),
        **extra,
    )


def held(space, *values):
    return [pltpu.with_memory_space_constraint(v, space) for v in values]


def near(*values):
    return held(pltpu.VMEM, *values)


def body(groups, lanes, queries, key_vectors, head_value_rows, out_gain):
    tokens, features = queries.shape
    if tokens != BLOCK or features != lanes * HEAD_DIM:
        raise ValueError("unsupported sizes")
    blocks = lanes
    _, nodes = node_offsets(blocks)
    one = (HEAD_DIM, HEAD_DIM)
    pair = (HEAD_DIM, 2 * HEAD_DIM)
    unit = 2 * BLOCK**3 * 4
    dma = pltpu.SemaphoreType.DMA
    (pieces,) = call(
        pack_kernel, "pack", [((lanes, 2, BLOCK, HEAD_DIM), bf16)], 0,
        scratch=[pltpu.VMEM((2, tokens, features), bf16), dma((2,))], in_space=[pltpu.HBM] * 2,
    )(*held(pltpu.HBM, key_vectors, head_value_rows))
    kv = lax.all_to_all(pieces, "lo", split_axis=0, concat_axis=0, tiled=True)
    a, b, total = call(
        functools.partial(maps_kernel, groups > 2), "maps",
        [((nodes, *pair), bf16), ((nodes, *one), f32), (one, bf16 if groups == 2 else f32)], unit * blocks * 20,
    )(*near(kv))
    hop = [(source, (source + 1) % groups) for source in range(groups)]
    incoming = lax.ppermute(total, "hi", hop)
    if groups > 2:
        top = a[nodes - 1].astype(f32)
        transition = top[:, :HEAD_DIM] + top[:, HEAD_DIM:]

        def relay(i, arriving):
            arriving = jnp.where(lax.axis_index("hi") > 0, arriving, 0.0)
            leaving = jnp.dot(transition, arriving, precision=lax.Precision.HIGHEST) + total
            return lax.ppermute(leaving, "hi", hop)

        incoming = lax.fori_loop(0, groups - 2, relay, incoming)
    pa, pb = call(
        sweep_kernel, "sweep", [((nodes, *pair), bf16), ((nodes, *one), f32)], unit * blocks * 2,
    )(*near(a, b))
    (states,) = call(
        states_kernel, "states", [((blocks, *one), bf16)], unit * blocks, kept=False,
        scratch=[pltpu.VMEM((blocks, *one), bf16), dma((PARTS,))],
    )(*near(pa, pb), incoming)
    states, queries, key_vectors, head_value_rows = lax.optimization_barrier(
        (states, queries, key_vectors, head_value_rows)
    )
    back = lax.all_to_all(states, "lo", split_axis=0, concat_axis=0, tiled=True)
    qt, ol = call(
        local_kernel, "local", [((lanes, *pair), bf16), ((lanes, *one), f32)], unit * blocks * 20,
        scratch=[pltpu.VMEM((3, tokens, features), bf16), dma((3,))], in_space=[pltpu.HBM] * 3,
    )(*held(pltpu.HBM, key_vectors, head_value_rows, queries))
    (mixed,) = call(
        final_kernel, "final", [((tokens, features), bf16)], unit * blocks, kept=False,
        scratch=[pltpu.VMEM((tokens, features), bf16), dma((PARTS,))],
    )(*near(qt, ol, back), out_gain.reshape(1, HEAD_DIM))
    return mixed


def solution(mesh):
    count = mesh.devices.size

    def run(queries, key_vectors, head_value_rows, out_gain):
        lanes = queries.shape[1] // HEAD_DIM
        regrouped = Mesh(mesh.devices.reshape(count // lanes, lanes), ("hi", "lo"))
        rows = P(("hi", "lo"), None)
        return jax.shard_map(
            functools.partial(body, count // lanes, lanes),
            mesh=regrouped, in_specs=(rows, rows, rows, P()), out_specs=rows, check_vma=False,
        )(queries, key_vectors, head_value_rows, out_gain)

    return run
```
